512 devices in a mesh: rows: 32 (over y, z_lo, core), cols: 16 (over x, z_hi).
Axes of the slice: x: 4, y: 4, z: 16 (z_hi: 4, z_lo: 4; z = z_hi * 4 + z_lo), core: 2. Of those that a mesh axis runs over, the one named last changes fastest.
Arguments:
- points: float32 [16384, 256], P('rows'), may hold values from -4 to 4, as said below
- centers: float32 [16384, 256], P('cols'), may hold values from -4 to 4, as said below
- inv_factor: float32 [16384, 16384], P('cols', 'rows'), may hold values from -2 to 2, as said below
- solution: float32 [16384, 128], P('rows'), may hold values from -6 to 6
- residual: float32 [16384, 128], P('rows'), may hold values from -40 to 40
- direction: float32 [16384, 128], P('rows'), may hold values from -40 to 40
Outputs:
- new_solution: float32 [16384, 128], P('rows')
- new_residual: float32 [16384, 128], P('rows')
- new_direction: float32 [16384, 128], P('rows')
The draws below stay inside these ranges and needn't reach their ends.
Inputs may be any that keep to these rules, and one draw needn't show every extreme that they name: `points`: each point's coordinates have a fixed spread that differs from coordinate to coordinate. `centers`: drawn by the same law as points. `inv_factor`: upper triangular with a positive diagonal.
All inputs are finite; a program needn't handle non-finite values.
Results may differ from the reference program's by a relative error of at most 0.00027.
Values sent between devices are 32-bit elements; how exact they have to be, the bound alone decides.
A program may use at most 64 MiB of HBM per device.

```python
import math
import jax
import jax.numpy as jnp
from jax import lax

D = 256
CENTERS = 16384
TARGETS = 128
ROWS_DEV = 512
POINTS = 16384
N_ROWS = 32


def spectrum_points(key, count):
    scales = jnp.sqrt(0.83 / (jnp.arange(D, dtype=jnp.float32) + 1.0))
    values = jnp.clip(jax.random.normal(key, (count, D), jnp.float32), -4.0, 4.0)
    return values * scales[None, :]


def draw_points(key, part):
    return spectrum_points(jax.random.fold_in(key, 11), POINTS)


def draw_centers(key, part):
    return spectrum_points(jax.random.fold_in(key, 23), CENTERS)


def draw_inv_factor(key, part):
    first_key, second_key = jax.random.split(jax.random.fold_in(key, 37))
    level = math.sqrt(250.0 / math.sqrt(POINTS * CENTERS))
    diagonal = level * jnp.exp(jax.random.uniform(first_key, (CENTERS,), jnp.float32, math.log(0.5), math.log(2.0)))
    upper_part = jnp.clip(jax.random.normal(second_key, (CENTERS, CENTERS), jnp.float32), -4.0, 4.0)
    upper_part = upper_part * (level / math.sqrt(CENTERS))
    return jnp.triu(upper_part, 1) + jnp.diag(diagonal)


def scaled_vector(key):
    first_key, second_key = jax.random.split(key, 2)
    row_scale = 0.3 * jnp.power(10.0, jnp.arange(CENTERS, dtype=jnp.float32) / CENTERS)
    col_scale = jnp.exp(jax.random.uniform(second_key, (TARGETS,), jnp.float32, math.log(0.3), math.log(3.0)))
    values = jnp.clip(jax.random.normal(first_key, (CENTERS, TARGETS), jnp.float32), -4.0, 4.0)
    return values * row_scale[:, None] * col_scale[None, :]


def draw_residual(key, part):
    return scaled_vector(jax.random.fold_in(key, 31))


def draw_direction(key, part):
    return scaled_vector(jax.random.fold_in(key, 47))


def level_of(own_key, extent, cuts, smallest, top_value):
    loudness, own = 1.0, jax.random.fold_in(own_key, 6)
    for position, parts in cuts:
        draws = jnp.exp(jax.random.uniform(jax.random.fold_in(own, position), (parts,), jnp.float32, smallest / len(cuts), top_value / len(cuts)))
        loudness = loudness * jnp.repeat(draws, extent[position] // parts).reshape([-1 if axis == position else 1 for axis in range(len(extent))])
    return loudness


def centred(rng, shape, scale, most, cuts=(), kind=jnp.bfloat16):
    result = scale * jax.random.normal(rng, shape, jnp.float32)
    if cuts:
        result = result * level_of(rng, shape, cuts, -0.22, 0.18)
    return jnp.clip(result, -most, most).astype(kind)


def setup_inputs(seed: int = 0) -> dict:
    seeds = jax.random.split(jax.random.key(seed), 7)
    return {
        "points": draw_points(jax.random.fold_in(seeds[6], 71), 0),
        "centers": draw_centers(jax.random.fold_in(seeds[6], 71), 0),
        "inv_factor": draw_inv_factor(jax.random.fold_in(seeds[6], 71), 0),
        "solution": centred(seeds[3], (CENTERS, TARGETS), 1.0, 6.0, ((0, 32),), jnp.float32),
        "residual": draw_residual(jax.random.fold_in(seeds[6], 71), 0),
        "direction": draw_direction(jax.random.fold_in(seeds[6], 71), 0),
    }


ridge_weight = 0.02


def reference(points, centers, inv_factor, solution, residual, direction):
    highest = lax.Precision.HIGHEST
    mapped = jnp.dot(inv_factor, direction, precision=highest, preferred_element_type=jnp.float32)
    center_sq = jnp.sum(centers * centers, axis=1)
    blocks = points.reshape(N_ROWS, ROWS_DEV, D)

    def add_block(accumulated, point_block):
        point_sq = jnp.sum(point_block * point_block, axis=1)
        inner_products = lax.dot_general(point_block, centers, (((1,), (1,)), ((), ())), precision=highest, preferred_element_type=jnp.float32)
        kernel = jnp.exp(-0.5 * ((point_sq[:, None] + center_sq[None, :]) - 2.0 * inner_products))
        predicted = jnp.dot(kernel, mapped, precision=highest, preferred_element_type=jnp.float32)
        back_part = lax.dot_general(kernel, predicted, (((0,), (0,)), ((), ())), precision=highest, preferred_element_type=jnp.float32)
        return accumulated + back_part, None

    back, unused = lax.scan(add_block, jnp.zeros((CENTERS, TARGETS), jnp.float32), blocks)
    image = lax.dot_general(inv_factor, back, (((0,), (0,)), ((), ())), precision=highest, preferred_element_type=jnp.float32) + ridge_weight * direction
    norm_now = jnp.sum(residual * residual, axis=0)
    curvature = jnp.sum(direction * image, axis=0)
    step_size = norm_now / curvature
    new_solution = solution + step_size[None, :] * direction
    new_residual = residual - step_size[None, :] * image
    norm_next = jnp.sum(new_residual * new_residual, axis=0)
    new_direction = new_residual + (norm_next / norm_now)[None, :] * direction
    return new_solution, new_residual, new_direction
```

```python
import functools

import jax
import jax.numpy as jnp
from jax import lax
from jax.experimental import pallas as pl
from jax.experimental.pallas import tpu as pltpu
from jax.sharding import PartitionSpec as P

ridge_weight = 0.02
MESH = pl.DeviceIdType.MESH
F32, BF16 = jnp.float32, jnp.bfloat16
T = 128
Q = 128


def split(a):
    high = a.astype(BF16)
    return high, (a - high.astype(F32)).astype(BF16)


def paired(a):
    return jnp.concatenate(split(a), axis=1)


def product(high, low, pair):
    both = jnp.dot(high, pair, preferred_element_type=F32) + jnp.dot(low, pair, preferred_element_type=F32)
    return both[:, :T] + both[:, T:]


def across(a, b, precision=lax.Precision.HIGHEST):
    return lax.dot_general(a, b, (((1,), (1,)), ((), ())), precision=precision, preferred_element_type=F32)


def rows_of(start, size):
    return pl.ds(pl.multiple_of(start, size), size)


def kernel(
    points, centers, factor, solution_, residual, direction,
    out_solution, out_residual, out_direction,
    away, own, core_in, y_in, z_in, full_c,
    part, x_in, zh_out, zh_in1, zh_in2, full_r,
    kh, kl, kth, ktl, rth, rtl,
    sm_out, sm_a, sm_z, sm_x,
    send, recv, send_s, recv_s,
):
    r, c = lax.axis_index("rows"), lax.axis_index("cols")
    y, zl, k = r // 8, (r // 2) % 4, r % 2
    x, zh = c // 4, c % 4

    def at(y_=None, zl_=None, k_=None, x_=None, zh_=None):
        pick = lambda new, old: old if new is None else new
        return (pick(y_, y) * 8 + pick(zl_, zl) * 2 + pick(k_, k), pick(x_, x) * 4 + pick(zh_, zh))

    sibling = at(k_=1 - k)
    ys = [at(y_=(y + j) % 4) for j in (1, 2, 3)]
    zls = [at(zl_=(zl + j) % 4) for j in (1, 2, 3)]
    xs = [at(x_=(x + j) % 4) for j in (1, 2, 3)]
    zh_a = at(zh_=zh + 1 - 2 * (zh % 2))
    zh_b = at(zh_=(zh + 3 - 2 * (zh % 2)) % 4)
    yk = y * 2 + k
    others = [(yk + j) % 8 for j in range(1, 8)]
    y_others = [at(y_=o // 2, k_=o % 2) for o in others]

    peers = zls + xs + [zh_a, zh_b] + y_others
    barrier = pltpu.get_barrier_semaphore()
    for p in peers:
        pl.semaphore_signal(barrier, inc=1, device_id=p, device_id_type=MESH)

    pending = []

    def copy(src, dst, s, d, device):
        return pltpu.make_async_remote_copy(
            src_ref=src, dst_ref=dst, send_sem=s, recv_sem=d, device_id=device, device_id_type=MESH
        )

    def push(src, dst, s, d, device):
        cp = copy(src, dst, s, d, device)
        cp.start()
        pending.append(cp)

    def arrived(dst, s, d):
        copy(dst, dst, s, d, sibling).wait_recv()

    def small_start(n, value):
        sm_a[n, yk] = value
        sm_out[n] = value
        for j, o in enumerate(y_others):
            push(sm_out.at[n], sm_a.at[n, yk], send_s.at[n, j], recv_s.at[n, yk], o)

    def small_middle(n):
        for j in range(7):
            arrived(sm_a.at[n, others[j]], send_s.at[n, j], recv_s.at[n, others[j]])
        total = sm_a[n, 0]
        for j in range(1, 8):
            total = total + sm_a[n, j]
        sm_z[n, zl] = total
        for j, o in enumerate(zls):
            push(sm_z.at[n, zl], sm_z.at[n, zl], send_s.at[n, 8 + j], recv_s.at[n, 8 + zl], o)

    def small_end(n):
        for j in (1, 2, 3):
            o = (zl + j) % 4
            arrived(sm_z.at[n, o], send_s.at[n, 8 + j - 1], recv_s.at[n, 8 + o])
        return (sm_z[n, 0] + sm_z[n, 1]) + (sm_z[n, 2] + sm_z[n, 3])

    def sum_over_rows(n, piece, ready, gaps):
        for q in range(4):
            away[n, q * Q : (q + 1) * Q] = piece((1 - k) * 512 + q * Q)
        ready()
        for q in range(4):
            rows = pl.ds(q * Q, Q)
            push(away.at[n, rows], core_in.at[n, rows], send.at[n, q], recv.at[n, q], sibling)
        for q in range(4):
            own[n, q * Q : (q + 1) * Q] = piece(k * 512 + q * Q)
        for j in (2, 1, 3, 0):
            q = (y + j) % 4
            rows = rows_of(q * Q, Q)
            arrived(core_in.at[n, rows], send.at[n, q], recv.at[n, q])
            own[n, rows] = own[n, rows] + core_in[n, rows]
            if j:
                push(own.at[n, rows], y_in.at[n, j - 1], send.at[n, 4 + j - 1], recv.at[n, 4 + j - 1], ys[j - 1])
        gaps[0]()
        mine = rows_of(y * Q, Q)
        for j in (1, 2, 3):
            arrived(y_in.at[n, j - 1], send.at[n, 4 + j - 1], recv.at[n, 4 + j - 1])
        z_in[n, zl] = (own[n, mine] + y_in[n, 0]) + (y_in[n, 1] + y_in[n, 2])
        for j in (3, 2, 1):
            push(z_in.at[n, zl], z_in.at[n, zl], send.at[n, 7 + j - 1], recv.at[n, 7 + zl], zls[j - 1])
        gaps[1]()
        for j in (1, 2, 3):
            o = (zl + j) % 4
            arrived(z_in.at[n, o], send.at[n, 7 + j - 1], recv.at[n, 7 + o])
        here = rows_of(k * 512 + y * Q, Q)
        full_c[n, here] = (z_in[n, 0] + z_in[n, 1]) + (z_in[n, 2] + z_in[n, 3])
        for j in (2, 1, 3):
            push(full_c.at[n, here], full_c.at[n, here], send.at[n, 11 + j - 1], recv.at[n, 11 + y], ys[j - 1])
        push(full_c.at[n, here], full_c.at[n, here], send.at[n, 15 + y], recv.at[n, 15 + y], sibling)
        gaps[2]()
        for j in (1, 3, 2):
            o = (y + j) % 4
            there = rows_of(k * 512 + o * Q, Q)
            arrived(full_c.at[n, there], send.at[n, 11 + j - 1], recv.at[n, 11 + o])
            push(full_c.at[n, there], full_c.at[n, there], send.at[n, 15 + o], recv.at[n, 15 + o], sibling)

    def sum_over_cols(n, high, low, gaps):
        mine, his = rows_of(k * 512, 512), rows_of((1 - k) * 512, 512)
        pair = paired(full_c[n, mine])
        for q in range(4):
            rows = pl.ds(q * Q, Q)
            part[n, rows] = product(high[rows, mine], low[rows, mine], pair)
        for o in range(4):
            there = rows_of((1 - k) * 512 + o * Q, Q)
            arrived(full_c.at[n, there], send.at[n, 15 + o], recv.at[n, 15 + o])
        pair = paired(full_c[n, his])
        for j in (2, 1, 3, 0):
            rows = rows_of((x + j) % 4 * Q, Q)
            part[n, rows] = part[n, rows] + product(high[rows, his], low[rows, his], pair)
            if j:
                push(part.at[n, rows], x_in.at[n, j - 1], send.at[n, 19 + j - 1], recv.at[n, 19 + j - 1], xs[j - 1])
        gaps[0]()
        here = rows_of(x * Q, Q)
        for j in (1, 2, 3):
            arrived(x_in.at[n, j - 1], send.at[n, 19 + j - 1], recv.at[n, 19 + j - 1])
        zh_out[n, 0] = (part[n, here] + x_in[n, 0]) + (x_in[n, 1] + x_in[n, 2])
        low_half, high_half = pl.ds(0, Q // 2), pl.ds(Q // 2, Q // 2)
        push(zh_out.at[n, 0, low_half], zh_in1.at[n, 0], send.at[n, 22], recv.at[n, 22], zh_a)
        push(zh_out.at[n, 0, high_half], zh_in1.at[n, 1], send.at[n, 23], recv.at[n, 23], zh_b)
        gaps[1]()
        arrived(zh_in1.at[n, 0], send.at[n, 22], recv.at[n, 22])
        zh_out[n, 1, low_half] = zh_out[n, 0, low_half] + zh_in1[n, 0]
        push(zh_out.at[n, 1, low_half], zh_in2.at[n, 0], send.at[n, 24], recv.at[n, 24], zh_b)
        arrived(zh_in1.at[n, 1], send.at[n, 23], recv.at[n, 23])
        zh_out[n, 1, high_half] = zh_out[n, 0, high_half] + zh_in1[n, 1]
        push(zh_out.at[n, 1, high_half], zh_in2.at[n, 1], send.at[n, 25], recv.at[n, 25], zh_a)
        gaps[2]()
        for half in (0, 1):
            arrived(zh_in2.at[n, half], send.at[n, 24 + half], recv.at[n, 24 + half])
        full_r[n, here] = zh_out[n, 1] + zh_in2[n].reshape(Q, T)
        for j in (2, 1, 3):
            push(full_r.at[n, here], full_r.at[n, here], send.at[n, 26 + j - 1], recv.at[n, 26 + x], xs[j - 1])
        gaps[3]()
        for j in (1, 3, 2):
            o = (x + j) % 4
            there = rows_of(o * Q, Q)
            arrived(full_r.at[n, there], send.at[n, 26 + j - 1], recv.at[n, 26 + o])

    def norms(a):
        return jnp.broadcast_to(jnp.sum(a * a, axis=0, keepdims=True), (8, T))

    def nothing():
        pass

    def kernel_rows(q, left, right, high, low):
        rows = pl.ds(q * Q, Q)
        a, b = left[rows, :], right[...]
        a_sq = jnp.sum(a * a, axis=1, keepdims=True)
        b_sq = across(jnp.ones((8, b.shape[1]), F32), b * b)[0:1]
        inner = across(a, b)
        high[rows, :], low[rows, :] = split(jnp.exp(-0.5 * ((a_sq + b_sq) - 2.0 * inner)))

    def some_kernel(which):
        def run():
            for q in which:
                kernel_rows(q, points, centers, kh, kl)

        return run

    def some_transposed(which):
        def run():
            for q in which:
                kernel_rows(q, centers, points, kth, ktl)

        return run

    def some_factor(which):
        def run():
            for q in which:
                rows = pl.ds(q * 256, 256)
                rth[:, q * 256 : (q + 1) * 256], rtl[:, q * 256 : (q + 1) * 256] = split(factor[rows, :].T)

        return run

    direction_pair = paired(direction[...])

    def mapped_piece(start):
        high, low = split(factor[rows_of(start, Q), :])
        return product(high, low, direction_pair)

    def entered():
        pl.semaphore_wait(barrier, len(peers))

    sum_over_rows(0, mapped_piece, entered, [some_kernel([0]), some_kernel([1, 2]), some_kernel([3])])
    sum_over_cols(
        0, kh, kl, [some_transposed([0]), some_transposed([1, 2, 3]), some_transposed([4, 5, 6]), some_transposed([7])]
    )

    predicted = full_r[0]
    predicted_pair = paired(predicted)
    lines = jnp.concatenate(
        [norms(residual[...])[0:1], norms(direction[...])[0:1], norms(predicted)[0:1], jnp.zeros((5, T), F32)], axis=0
    )

    def back_piece(start):
        rows = rows_of(start, Q)
        return product(kth[rows, :], ktl[rows, :], predicted_pair)

    def first_norms():
        some_factor([0])()
        small_start(0, lines)

    def second_norms():
        some_factor([1, 2])()
        small_middle(0)

    sum_over_rows(1, back_piece, nothing, [first_norms, second_norms, some_factor([3])])
    sum_over_cols(1, rth, rtl, [nothing] * 4)

    sums = small_end(0)
    norm_now = sums[0:1]
    step_size = norm_now / (sums[2:3] + ridge_weight * sums[1:2])
    old = direction[...]
    out_solution[...] = solution_[...] + step_size * old
    new_residual = residual[...] - step_size * (full_r[1] + ridge_weight * old)
    out_residual[...] = new_residual
    small_start(1, norms(new_residual))
    small_middle(1)
    norm_next = small_end(1)[0:1]
    out_direction[...] = new_residual + (norm_next / norm_now) * old
    for cp in pending:
        cp.wait_send()


def body(points, centers, factor, solution_, residual, direction):
    vmem = pl.BlockSpec(memory_space=pltpu.VMEM)
    out = jax.ShapeDtypeStruct(solution_.shape, F32)
    dma = pltpu.SemaphoreType.DMA
    v = lambda *shape: pltpu.VMEM(shape, F32)
    h = lambda *shape: pltpu.VMEM(shape, BF16)
    return pl.pallas_call(
        kernel,
        name="cg_iteration",
        out_shape=(out, out, out),
        in_specs=[vmem] * 6,
        out_specs=(vmem,) * 3,
        scratch_shapes=[
            v(2, 512, T), v(2, 512, T), v(2, 512, T), v(2, 3, Q, T), v(2, 4, Q, T), v(2, 1024, T),
            v(2, 512, T), v(2, 3, Q, T), v(2, 2, Q, T), v(2, 2, Q // 2, T), v(2, 2, Q // 2, T), v(2, 512, T),
            h(512, 1024), h(512, 1024), h(1024, 512), h(1024, 512), h(512, 1024), h(512, 1024),
            v(2, 8, T), v(2, 8, 8, T), v(2, 4, 8, T), v(2, 4, 8, T),
            dma((2, 32)), dma((2, 32)), dma((2, 16)), dma((2, 16)),
        ],
        compiler_params=pltpu.CompilerParams(collective_id=0, has_side_effects=True, vmem_limit_bytes=60 * 2**20),
    )(points, centers, factor, solution_, residual, direction)


def solution(mesh):
    return jax.shard_map(
        body,
        mesh=mesh,
        in_specs=(
            P("rows", None),
            P("cols", None),
            P("cols", "rows"),
            P("rows", None),
            P("rows", None),
            P("rows", None),
        ),
        out_specs=(P("rows", None), P("rows", None), P("rows", None)),
        check_vma=False,
    )
```

```python
import jax
import jax.numpy as jnp
from jax import lax
from jax.experimental import pallas as pl
from jax.experimental.pallas import tpu as pltpu
from jax.sharding import PartitionSpec as P

ridge_weight = 0.02
MESH = pl.DeviceIdType.MESH
F32, BF16 = jnp.float32, jnp.bfloat16
T = 128
W = 64
Q = 128
H = 64


def split(a):
    high = a.astype(BF16)
    return high, (a - high.astype(F32)).astype(BF16)


def swap(a):
    return pltpu.roll(a, W, 1)


def first_lanes(rows):
    return lax.broadcasted_iota(jnp.int32, (rows, T), 1) < W


def pack(full, chain):
    top, bottom = full[:H], full[H:]
    if chain == 0:
        return jnp.where(first_lanes(H), top, swap(bottom))
    return jnp.where(first_lanes(H), swap(top), bottom)


def unpack(a, b):
    m = first_lanes(H)
    return jnp.concatenate([jnp.where(m, a, swap(b)), jnp.where(m, swap(a), b)], axis=0)


def fold(both):
    total = both + swap(both)
    return jnp.where(first_lanes(H), total[:H], total[H:])


def operand(packed):
    high = packed.astype(BF16).astype(F32)
    low = packed - high
    m = first_lanes(H)
    return jnp.concatenate([jnp.where(m, high, swap(low)), jnp.where(m, swap(high), low)], axis=0).astype(BF16)


def dot(a, b):
    return jnp.dot(a, b, preferred_element_type=F32)


def across(a, b):
    return lax.dot_general(
        a, b, (((1,), (1,)), ((), ())), precision=lax.Precision.HIGHEST, preferred_element_type=F32
    )


def rows_of(start, size):
    return pl.ds(pl.multiple_of(start, size), size)


def kernel(
    points_, centers_, factor_, residual_, direction_,
    image_, step_out, ratio_out,
    points, centers, factor, residual, direction, image,
    away, own, core_in, y_in, z_in, full_c,
    part, x_in, zh_out, zh_in1, zh_in2, full_r,
    kh, kl, kth, ktl, rth, rtl,
    sm_out, sm_a, sm_b,
    send, recv, send_s, recv_s, local,
):
    r, c = lax.axis_index("rows"), lax.axis_index("cols")
    y, zl, k = r // 8, (r // 2) % 4, r % 2
    x, zh = c // 4, c % 4

    def at(y_=None, zl_=None, k_=None, x_=None, zh_=None):
        pick = lambda new, old: old if new is None else new
        return (pick(y_, y) * 8 + pick(zl_, zl) * 2 + pick(k_, k), pick(x_, x) * 4 + pick(zh_, zh))

    sibling = at(k_=1 - k)
    ys = [at(y_=(y + j) % 4) for j in (1, 2, 3)]
    zls = [at(zl_=(zl + j) % 4) for j in (1, 2, 3)]
    xs = [at(x_=(x + j) % 4) for j in (1, 2, 3)]
    zh_a = at(zh_=zh + 1 - 2 * (zh % 2))
    zh_b = at(zh_=(zh + 3 - 2 * (zh % 2)) % 4)
    xk, yz = x * 2 + k, y * 4 + zl
    other_xk = [(x + j) % 4 * 2 + (k + e) % 2 for j in range(4) for e in range(2)][1:]
    other_yz = [(y + j) % 4 * 4 + (zl + e) % 4 for j in range(4) for e in range(4)][1:]
    xks = [at(x_=o // 2, k_=o % 2) for o in other_xk]
    yzs = [at(y_=o // 4, zl_=o % 4) for o in other_yz]

    peers = [zh_a, zh_b] + yzs + xks
    barrier = pltpu.get_barrier_semaphore()
    for p in peers:
        pl.semaphore_signal(barrier, inc=1, device_id=p, device_id_type=MESH)

    here_half, there_half = rows_of(k * 512, 512), rows_of((1 - k) * 512, 512)
    loads = [
        pltpu.make_async_copy(a, b, local.at[i])
        for i, (a, b) in enumerate(
            [
                (direction_, direction),
                (factor_.at[there_half], factor.at[there_half]),
                (factor_.at[here_half], factor.at[here_half]),
                (centers_, centers),
                (points_, points),
                (residual_, residual),
            ]
        )
    ]
    for load in loads:
        load.start()

    pending = []

    def copy(src, dst, s, d, device):
        return pltpu.make_async_remote_copy(
            src_ref=src, dst_ref=dst, send_sem=s, recv_sem=d, device_id=device, device_id_type=MESH
        )

    def push(src, dst, s, d, device):
        cp = copy(src, dst, s, d, device)
        cp.start()
        pending.append(cp)

    def arrived(dst, s, d):
        copy(dst, dst, s, d, sibling).wait_recv()

    def small_start(n, value, slot, slots, devices):
        sm_a[n, slot] = value
        sm_out[n] = value
        for j, device in enumerate(devices):
            push(sm_out.at[n], sm_a.at[n, slot], send_s.at[n, j], recv_s.at[n, slot], device)

    def small_middle(n, slots, count):
        for j, o in enumerate(slots):
            arrived(sm_a.at[n, o], send_s.at[n, j], recv_s.at[n, o])
        total = sm_a[n, 0]
        for j in range(1, count):
            total = total + sm_a[n, j]
        sm_b[n, yz] = total
        for j, device in enumerate(yzs):
            push(sm_b.at[n, yz], sm_b.at[n, yz], send_s.at[n, 8 + j], recv_s.at[n, 8 + yz], device)

    def small_end(n):
        for j, o in enumerate(other_yz):
            arrived(sm_b.at[n, o], send_s.at[n, 8 + j], recv_s.at[n, 8 + o])
        total = sm_b[n, 0]
        for j in range(1, 16):
            total = total + sm_b[n, j]
        return total

    def send_away(s):
        for q in range(4):
            rows = pl.ds(q * H, H)
            push(away.at[s, rows], core_in.at[s, rows], send.at[s, q], recv.at[s, q], sibling)

    def chain(p, n, high, low):
        s = 2 * n + p
        yield
        for j in (2, 1, 3, 0):
            q = (y + j) % 4
            rows = rows_of(q * H, H)
            arrived(core_in.at[s, rows], send.at[s, q], recv.at[s, q])
            own[s, rows] = own[s, rows] + core_in[s, rows]
            if j:
                push(own.at[s, rows], y_in.at[s, j - 1], send.at[s, 4 + j - 1], recv.at[s, 4 + j - 1], ys[j - 1])
        yield
        mine = rows_of(y * H, H)
        for j in (1, 3, 2):
            arrived(y_in.at[s, j - 1], send.at[s, 4 + j - 1], recv.at[s, 4 + j - 1])
        z_in[s, zl] = (own[s, mine] + y_in[s, 0]) + (y_in[s, 1] + y_in[s, 2])
        for j in (2, 1, 3):
            push(z_in.at[s, zl], z_in.at[s, zl], send.at[s, 7 + j - 1], recv.at[s, 7 + zl], zls[j - 1])
        yield
        for j in (1, 3, 2):
            o = (zl + j) % 4
            arrived(z_in.at[s, o], send.at[s, 7 + j - 1], recv.at[s, 7 + o])
        here = rows_of(k * 256 + y * H, H)
        full_c[s, here] = (z_in[s, 0] + z_in[s, 1]) + (z_in[s, 2] + z_in[s, 3])
        for j in (2, 1, 3):
            push(full_c.at[s, here], full_c.at[s, here], send.at[s, 11 + j - 1], recv.at[s, 11 + y], ys[j - 1])
        push(full_c.at[s, here], full_c.at[s, here], send.at[s, 15 + y], recv.at[s, 15 + y], sibling)
        yield
        for j in (1, 3, 2):
            o = (y + j) % 4
            there = rows_of(k * 256 + o * H, H)
            arrived(full_c.at[s, there], send.at[s, 11 + j - 1], recv.at[s, 11 + o])
            push(full_c.at[s, there], full_c.at[s, there], send.at[s, 15 + o], recv.at[s, 15 + o], sibling)
        mine, his = rows_of(k * 512, 512), rows_of((1 - k) * 512, 512)

        def half(base):
            return jnp.concatenate([operand(full_c[s, rows_of(base * 256 + q * H, H)]) for q in range(4)], axis=0)

        b = half(k)
        for q in range(4):
            rows = pl.ds(q * Q, Q)
            part[s, rows] = dot(high[rows, mine], b) + dot(low[rows, mine], b)
        yield
        for o in range(4):
            there = rows_of((1 - k) * 256 + o * H, H)
            arrived(full_c.at[s, there], send.at[s, 15 + o], recv.at[s, 15 + o])
        b = half(1 - k)
        for j in (2, 1, 3, 0):
            q = (x + j) % 4
            rows = rows_of(q * Q, Q)
            slot = zh_out.at[s, 0] if j == 0 else zh_out.at[s, 1 + j]
            slot[...] = fold(part[s, rows] + (dot(high[rows, his], b) + dot(low[rows, his], b)))
            if j:
                push(slot, x_in.at[s, j - 1], send.at[s, 19 + j - 1], recv.at[s, 19 + j - 1], xs[j - 1])
        yield
        for j in (1, 3, 2):
            arrived(x_in.at[s, j - 1], send.at[s, 19 + j - 1], recv.at[s, 19 + j - 1])
        zh_out[s, 0] = (zh_out[s, 0] + x_in[s, 0]) + (x_in[s, 1] + x_in[s, 2])
        first, second = pl.ds(0, H // 2), pl.ds(H // 2, H // 2)
        push(zh_out.at[s, 0, first], zh_in1.at[s, 0], send.at[s, 22], recv.at[s, 22], zh_a)
        push(zh_out.at[s, 0, second], zh_in1.at[s, 1], send.at[s, 23], recv.at[s, 23], zh_b)
        yield
        arrived(zh_in1.at[s, 0], send.at[s, 22], recv.at[s, 22])
        zh_out[s, 1, first] = zh_out[s, 0, first] + zh_in1[s, 0]
        push(zh_out.at[s, 1, first], zh_in2.at[s, 0], send.at[s, 24], recv.at[s, 24], zh_b)
        arrived(zh_in1.at[s, 1], send.at[s, 23], recv.at[s, 23])
        zh_out[s, 1, second] = zh_out[s, 0, second] + zh_in1[s, 1]
        push(zh_out.at[s, 1, second], zh_in2.at[s, 1], send.at[s, 25], recv.at[s, 25], zh_a)
        yield
        here = rows_of(x * H, H)
        for e in (0, 1):
            arrived(zh_in2.at[s, e], send.at[s, 24 + e], recv.at[s, 24 + e])
        full_r[s, here] = zh_out[s, 1] + zh_in2[s].reshape(H, T)
        for j in (2, 1, 3):
            push(full_r.at[s, here], full_r.at[s, here], send.at[s, 26 + j - 1], recv.at[s, 26 + x], xs[j - 1])
        yield
        for j in (1, 3, 2):
            o = (x + j) % 4
            there = rows_of(o * H, H)
            arrived(full_r.at[s, there], send.at[s, 26 + j - 1], recv.at[s, 26 + o])

    def back_terms(p):
        s = 2 + p
        b = jnp.concatenate([operand(full_r[p, q * H : (q + 1) * H]) for q in range(4)], axis=0)
        for q in range(4):
            rows = rows_of((1 - k) * 512 + q * Q, Q)
            away[s, q * H : (q + 1) * H] = fold(dot(kth[rows, :], b) + dot(ktl[rows, :], b))
        send_away(s)
        for q in range(4):
            rows = rows_of(k * 512 + q * Q, Q)
            own[s, q * H : (q + 1) * H] = fold(dot(kth[rows, :], b) + dot(ktl[rows, :], b))

    def whole(p):
        yield from chain(p, 0, kh, kl)
        back_terms(p)
        yield from chain(p, 1, rth, rtl)

    def kernel_block(e):
        def run():
            if e == 0:
                loads[3].wait()
                loads[4].wait()
            cols = slice(e * 256, (e + 1) * 256)
            a, b = points[...], centers[cols, :]
            a_sq = jnp.sum(a * a, axis=1, keepdims=True)
            b_sq = across(jnp.ones((8, b.shape[1]), F32), b * b)[0:1]
            block = jnp.exp(-0.5 * ((a_sq + b_sq) - 2.0 * across(a, b)))
            kh[:, cols], kl[:, cols] = split(block)
            kth[cols, :], ktl[cols, :] = split(block.T)

        return run

    def factor_block(e):
        def run():
            cols = slice(e * 256, (e + 1) * 256)
            rth[:, cols], rtl[:, cols] = split(factor[cols, :].T)

        return run

    def norm(a):
        return jnp.sum(a * a, axis=0, keepdims=True)

    def first_norms():
        loads[5].wait()
        squares = [norm(full_r[p]) for p in (0, 1)]
        squares = [a + swap(a) for a in squares]
        predicted = jnp.where(first_lanes(1), squares[0], squares[1])
        lines = [norm(residual[...]), norm(direction[...]), predicted, jnp.zeros((5, T), F32)]
        small_start(0, jnp.concatenate(lines, axis=0), k, [1 - k], [sibling])

    def second_norms():
        small_middle(0, [1 - k], 2)

    loads[0].wait()
    pair = jnp.concatenate(split(direction[...]), axis=1)

    def mapped(base, target):
        for q in range(4):
            high, low = split(factor[rows_of(base * 512 + q * Q, Q), :])
            both = dot(high, pair) + dot(low, pair)
            both = both[:, :T] + both[:, T:]
            for p in (0, 1):
                target[p, q * H : (q + 1) * H] = pack(both, p)

    loads[1].wait()
    mapped(1 - k, away)
    pl.semaphore_wait(barrier, len(peers))
    for p in (0, 1):
        send_away(p)
    loads[2].wait()
    mapped(k, own)

    chains = [whole(0), whole(1)]
    extra = {
        1: [kernel_block(0)],
        2: [kernel_block(1), kernel_block(2)],
        3: [kernel_block(3)],
        6: [factor_block(0), factor_block(1)],
        7: [factor_block(2), factor_block(3)],
        10: [first_norms],
        12: [second_norms],
    }
    for step in range(18):
        for p in (0, 1):
            next(chains[p])
        for run in extra.get(step, []):
            run()

    sums = small_end(0)
    norm_now = sums[0:1]
    step_size = norm_now / (sums[2:3] + ridge_weight * sums[1:2])
    quarter = rows_of(x * Q, Q)
    packed = rows_of(x * H, H)
    fresh = residual[quarter, :] - step_size * (
        unpack(full_r[2, packed], full_r[3, packed]) + ridge_weight * direction[quarter, :]
    )
    small_start(1, jnp.broadcast_to(norm(fresh), (8, T)), xk, other_xk, xks)
    for p in (0, 1):
        for unused in chains[p]:
            pass
    for q in range(4):
        rows = pl.ds(q * H, H)
        image[q * Q : (q + 1) * Q] = unpack(full_r[2, rows], full_r[3, rows])
    out = pltpu.make_async_copy(image, image_, local.at[6])
    out.start()
    small_middle(1, other_xk, 8)
    norm_next = small_end(1)[0:1]
    step_out[...] = step_size
    ratio_out[...] = norm_next / norm_now
    for cp in pending:
        cp.wait_send()
    out.wait()


def body(points, centers, factor, solution_, residual, direction):
    vmem, anywhere = pl.BlockSpec(memory_space=pltpu.VMEM), pl.BlockSpec(memory_space=pl.ANY)
    dma = pltpu.SemaphoreType.DMA
    v = lambda *shape: pltpu.VMEM(shape, F32)
    h = lambda *shape: pltpu.VMEM(shape, BF16)
    image, step_size, ratio = pl.pallas_call(
        kernel,
        name="cg_iteration",
        out_shape=(jax.ShapeDtypeStruct(direction.shape, F32), jax.ShapeDtypeStruct((1, T), F32), jax.ShapeDtypeStruct((1, T), F32)),
        in_specs=[anywhere] * 5,
        out_specs=(anywhere, vmem, vmem),
        scratch_shapes=[
            v(512, 256), v(1024, 256), v(1024, 512), v(512, T), v(512, T), v(512, T),
            v(4, 256, T), v(4, 256, T), v(4, 256, T), v(4, 3, H, T), v(4, 4, H, T), v(4, 512, T),
            v(4, 512, T), v(4, 3, H, T), v(4, 5, H, T), v(4, 2, H // 2, T), v(4, 2, H // 2, T), v(4, 256, T),
            h(512, 1024), h(512, 1024), h(1024, 512), h(1024, 512), h(512, 1024), h(512, 1024),
            v(2, 8, T), v(2, 8, 8, T), v(2, 16, 8, T),
            dma((4, 32)), dma((4, 32)), dma((2, 24)), dma((2, 24)), dma((8,)),
        ],
        compiler_params=pltpu.CompilerParams(collective_id=0, has_side_effects=True, vmem_limit_bytes=60 * 2**20),
    )(points, centers, factor, residual, direction)
    new_solution = solution_ + step_size * direction
    new_residual = residual - step_size * (image + ridge_weight * direction)
    return new_solution, new_residual, new_residual + ratio * direction


def solution(mesh):
    return jax.shard_map(
        body,
        mesh=mesh,
        in_specs=(
            P("rows", None),
            P("cols", None),
            P("cols", "rows"),
            P("rows", None),
            P("rows", None),
            P("rows", None),
        ),
        out_specs=(P("rows", None), P("rows", None), P("rows", None)),
        check_vma=False,
    )
```

```python
import jax
import jax.numpy as jnp
from jax import lax
from jax.experimental import pallas as pl
from jax.experimental.pallas import tpu as pltpu
from jax.sharding import PartitionSpec as P

ridge_weight = 0.02
MESH = pl.DeviceIdType.MESH
F32, BF16 = jnp.float32, jnp.bfloat16
T = 128
W = 64
Q = 128
H = 64


def split(a):
    high = a.astype(BF16)
    return high, (a - high.astype(F32)).astype(BF16)


def swap(a):
    return pltpu.roll(a, W, 1)


def first_lanes(rows):
    return lax.broadcasted_iota(jnp.int32, (rows, T), 1) < W


def pack(full, chain):
    top, bottom = full[:H], full[H:]
    if chain == 0:
        return jnp.where(first_lanes(H), top, swap(bottom))
    return jnp.where(first_lanes(H), swap(top), bottom)


def unpack(a, b):
    m = first_lanes(H)
    return jnp.concatenate([jnp.where(m, a, swap(b)), jnp.where(m, swap(a), b)], axis=0)


def fold(both):
    total = both + swap(both)
    return jnp.where(first_lanes(H), total[:H], total[H:])


def operand(packed):
    high = packed.astype(BF16).astype(F32)
    low = packed - high
    m = first_lanes(H)
    return jnp.concatenate([jnp.where(m, high, swap(low)), jnp.where(m, swap(high), low)], axis=0).astype(BF16)


def dot(a, b):
    return jnp.dot(a, b, preferred_element_type=F32)


def across(a, b):
    return lax.dot_general(
        a, b, (((1,), (1,)), ((), ())), precision=lax.Precision.HIGHEST, preferred_element_type=F32
    )


def rows_of(start, size):
    return pl.ds(pl.multiple_of(start, size), size)


def kernel(
    points_, centers_, factor_, residual_, direction_,
    image_, step_out, ratio_out,
    points, centers, factor, residual, direction, image,
    away, own, core_in, a_in, b_in, full_c,
    part, x_in, zh_out, zh_in1, zh_in2, full_r,
    kh, kl, kth, ktl, rth, rtl,
    small_a, small_b, line,
    send, recv, small_send, small_recv, local,
):
    r, c = lax.axis_index("rows"), lax.axis_index("cols")
    y, zl, k = r // 8, (r // 2) % 4, r % 2
    x, zh = c // 4, c % 4

    def at(y_=None, zl_=None, k_=None, x_=None, zh_=None):
        pick = lambda new, old: old if new is None else new
        return (pick(y_, y) * 8 + pick(zl_, zl) * 2 + pick(k_, k), pick(x_, x) * 4 + pick(zh_, zh))

    sibling = at(k_=1 - k)
    ys = [at(y_=(y + j) % 4) for j in (1, 2, 3)]
    zls = [at(zl_=(zl + j) % 4) for j in (1, 2, 3)]
    xs = [at(x_=(x + j) % 4) for j in (1, 2, 3)]
    zh_a = at(zh_=zh + 1 - 2 * (zh % 2))
    zh_b = at(zh_=(zh + 3 - 2 * (zh % 2)) % 4)
    column = [at((y + i) % 4, (zl + j) % 4, (k + e) % 2) for i in (2, 1, 3, 0) for j in (2, 1, 3, 0) for e in (1, 0)][:-1]

    here_half, there_half = rows_of(k * 512, 512), rows_of((1 - k) * 512, 512)
    loads = [
        pltpu.make_async_copy(a, b, local.at[i])
        for i, (a, b) in enumerate(
            [
                (direction_, direction),
                (factor_.at[there_half], factor.at[there_half]),
                (factor_.at[here_half], factor.at[here_half]),
                (centers_, centers),
                (points_, points),
                (residual_, residual),
            ]
        )
    ]
    loads[0].start()
    loads[1].start()

    peers = [zh_a, zh_b] + column + xs
    barrier = pltpu.get_barrier_semaphore()
    for p in peers:
        pl.semaphore_signal(barrier, inc=1, device_id=p, device_id_type=MESH)

    for load in loads[2:]:
        load.start()

    def copy(src, dst, s, d, device):
        return pltpu.make_async_remote_copy(
            src_ref=src, dst_ref=dst, send_sem=s, recv_sem=d, device_id=device, device_id_type=MESH
        )

    small = [small_a, small_b]

    def push(src, dst, s, phase, d, device):
        copy(src, dst, send.at[s % 2, phase], recv.at[s, d], device).start()

    def arrived(like, s, d):
        copy(like, like, send.at[s % 2, 0], recv.at[s, d], sibling).wait_recv()

    def sent(s, phase):
        like = {0: away, 4: away, 6: zh_in1, 7: zh_in2}.get(phase, a_in).at[s]
        copy(like, like, send.at[s % 2, phase], recv.at[s, 0], sibling).wait_send()

    def small_start(n, value):
        lines = small[n]
        lines[r] = value
        for device in column:
            copy(lines.at[r], lines.at[r], small_send.at[n], small_recv.at[n], device).start()

    def small_end(n):
        like = small[n].at[pl.ds(0, 31)]
        copy(like, like, small_send.at[n], small_recv.at[n], sibling).wait()
        return jnp.sum(small[n][...], axis=0)

    def send_away(s):
        if s > 1:
            sent(s, 0)
        for q in range(4):
            rows = pl.ds(q * H, H)
            push(away.at[s, rows], core_in.at[s, rows], s, 0, q, sibling)

    def chain(p, n, high, low):
        s = 2 * n + p
        (a, a_devices), (b, b_devices) = [((y, ys), (zl, zls)), ((zl, zls), (y, ys))][p]

        def again(*phases):
            for phase in phases if n else ():
                sent(s, phase)

        yield
        again(1)
        for j in (2, 1, 3, 0):
            q = (a + j) % 4
            rows = rows_of(q * H, H)
            arrived(core_in.at[s, rows], s, q)
            own[s, rows] = own[s, rows] + core_in[s, rows]
            if j:
                push(own.at[s, rows], a_in.at[s, j - 1], s, 1, 4, a_devices[j - 1])
        again(2)
        yield
        mine = rows_of(a * H, H)
        arrived(a_in.at[s], s, 4)
        b_in[s, b] = (own[s, mine] + a_in[s, 0]) + (a_in[s, 1] + a_in[s, 2])
        for j in (2, 1, 3):
            push(b_in.at[s, b], b_in.at[s, b], s, 2, 5, b_devices[j - 1])
        again(3, 4)
        yield
        arrived(a_in.at[s], s, 5)
        here = rows_of(k * 256 + a * H, H)
        full_c[s, here] = (b_in[s, 0] + b_in[s, 1]) + (b_in[s, 2] + b_in[s, 3])
        for j in (2, 1, 3):
            push(full_c.at[s, here], full_c.at[s, here], s, 3, 6 + j - 1, a_devices[j - 1])
        push(full_c.at[s, here], full_c.at[s, here], s, 4, 9, sibling)
        yield
        for j in (1, 3, 2):
            there = rows_of(k * 256 + (a + 4 - j) % 4 * H, H)
            arrived(full_c.at[s, there], s, 6 + j - 1)
            push(full_c.at[s, there], full_c.at[s, there], s, 4, 9, sibling)
        mine, his = rows_of(k * 512, 512), rows_of((1 - k) * 512, 512)

        def half(base):
            return jnp.concatenate([operand(full_c[s, rows_of(base * 256 + q * H, H)]) for q in range(4)], axis=0)

        term = half(k)
        for q in range(4):
            rows = pl.ds(q * Q, Q)
            part[s, rows] = dot(high[rows, mine], term) + dot(low[rows, mine], term)
        again(5)
        yield
        arrived(full_c.at[s, rows_of((1 - k) * 256, 256)], s, 9)
        term = half(1 - k)
        slots = [zh_out.at[s, 0], zh_out.at[s, 2], zh_out.at[s, 3], zh_out.at[s, 4]]
        for j in range(4):
            rows = rows_of((x + j) % 4 * Q, Q)
            slots[j][...] = fold(part[s, rows] + (dot(high[rows, his], term) + dot(low[rows, his], term)))
        for j in (2, 1, 3):
            push(slots[j], x_in.at[s, j - 1], s, 5, 10, xs[j - 1])
        again(6, 7)
        yield
        arrived(x_in.at[s], s, 10)
        zh_out[s, 0] = (zh_out[s, 0] + x_in[s, 0]) + (x_in[s, 1] + x_in[s, 2])
        first, second = pl.ds(0, H // 2), pl.ds(H // 2, H // 2)
        push(zh_out.at[s, 0, first], zh_in1.at[s, 0], s, 6, 11, zh_a)
        push(zh_out.at[s, 0, second], zh_in1.at[s, 1], s, 6, 12, zh_b)
        yield
        arrived(zh_in1.at[s, 0], s, 11)
        zh_out[s, 1, first] = zh_out[s, 0, first] + zh_in1[s, 0]
        push(zh_out.at[s, 1, first], zh_in2.at[s, 0], s, 7, 13, zh_b)
        arrived(zh_in1.at[s, 1], s, 12)
        zh_out[s, 1, second] = zh_out[s, 0, second] + zh_in1[s, 1]
        push(zh_out.at[s, 1, second], zh_in2.at[s, 1], s, 7, 13, zh_a)
        again(8)
        yield
        here = rows_of(x * H, H)
        arrived(zh_in2.at[s], s, 13)
        full_r[s, here] = zh_out[s, 1] + zh_in2[s].reshape(H, T)
        for j in (2, 1, 3):
            push(full_r.at[s, here], full_r.at[s, here], s, 8, 14, xs[j - 1])
        yield
        arrived(x_in.at[s], s, 14)

    def back_terms(p):
        s = 2 + p
        b = jnp.concatenate([operand(full_r[p, q * H : (q + 1) * H]) for q in range(4)], axis=0)
        for q in range(4):
            rows = rows_of((1 - k) * 512 + q * Q, Q)
            away[s, q * H : (q + 1) * H] = fold(dot(kth[rows, :], b) + dot(ktl[rows, :], b))
        send_away(s)
        for q in range(4):
            rows = rows_of(k * 512 + q * Q, Q)
            own[s, q * H : (q + 1) * H] = fold(dot(kth[rows, :], b) + dot(ktl[rows, :], b))

    def whole(p):
        yield from chain(p, 0, kh, kl)
        back_terms(p)
        yield from chain(p, 1, rth, rtl)

    def kernel_block(e):
        def run():
            if e == 0:
                loads[3].wait()
                loads[4].wait()
            cols = slice(e * 256, (e + 1) * 256)
            a, b = points[...], centers[cols, :]
            a_sq = jnp.sum(a * a, axis=1, keepdims=True)
            b_sq = across(jnp.ones((8, b.shape[1]), F32), b * b)[0:1]
            block = jnp.exp(-0.5 * ((a_sq + b_sq) - 2.0 * across(a, b)))
            kh[:, cols], kl[:, cols] = split(block)
            kth[cols, :], ktl[cols, :] = split(block.T)

        return run

    def factor_block(e):
        def run():
            cols = slice(e * 256, (e + 1) * 256)
            rth[:, cols], rtl[:, cols] = split(factor[cols, :].T)

        return run

    def norm(a):
        return jnp.sum(a * a, axis=0, keepdims=True)

    def first_norms():
        loads[5].wait()
        squares = [norm(full_r[p]) for p in (0, 1)]
        squares = [a + swap(a) for a in squares]
        predicted = jnp.where(first_lanes(1), squares[0], squares[1])
        small_start(0, jnp.concatenate([norm(residual[...]), norm(direction[...]), predicted], axis=1))

    loads[0].wait()
    pair = jnp.concatenate(split(direction[...]), axis=1)

    def mapped(base, target):
        for q in range(4):
            high, low = split(factor[rows_of(base * 512 + q * Q, Q), :])
            both = dot(high, pair) + dot(low, pair)
            both = both[:, :T] + both[:, T:]
            for p in (0, 1):
                target[p, q * H : (q + 1) * H] = pack(both, p)

    loads[1].wait()
    mapped(1 - k, away)
    pl.semaphore_wait(barrier, len(peers))
    for p in (0, 1):
        send_away(p)
    loads[2].wait()
    mapped(k, own)

    chains = [whole(0), whole(1)]
    extra = {
        1: [kernel_block(0), kernel_block(1)],
        2: [kernel_block(2), kernel_block(3)],
        6: [factor_block(0), factor_block(1)],
        7: [factor_block(2), factor_block(3)],
        10: [first_norms],
    }
    for step in range(18):
        for p in (0, 1):
            next(chains[p])
        for run in extra.get(step, []):
            run()

    sums = small_end(0)
    norm_now = sums[:, :T]
    step_size = norm_now / (sums[:, 2 * T :] + ridge_weight * sums[:, T : 2 * T])
    line[0] = step_size
    outs = [pltpu.make_async_copy(line.at[0], step_out, local.at[6])]
    outs[0].start()
    for p in (0, 1):
        for unused in chains[p]:
            pass
    total = jnp.zeros((1, T), F32)
    for q in range(4):
        rows, packed = slice(q * Q, (q + 1) * Q), pl.ds(q * H, H)
        quarter = unpack(full_r[2, packed], full_r[3, packed])
        image[rows] = quarter
        total = total + norm(residual[rows] - step_size * (quarter + ridge_weight * direction[rows]))
    small_start(1, total)
    outs.append(pltpu.make_async_copy(image, image_, local.at[7]))
    outs[1].start()
    for p in (0, 1):
        for phase in range(9):
            sent(2 + p, phase)
    for out in outs:
        out.wait()
    line[1] = small_end(1) / norm_now
    last = pltpu.make_async_copy(line.at[1], ratio_out, local.at[8])
    last.start()
    last.wait()


def body(points, centers, factor, solution_, residual, direction):
    anywhere = pl.BlockSpec(memory_space=pl.ANY)
    dma = pltpu.SemaphoreType.DMA
    v = lambda *shape: pltpu.VMEM(shape, F32)
    h = lambda *shape: pltpu.VMEM(shape, BF16)
    image, step_size, ratio = pl.pallas_call(
        kernel,
        name="cg_iteration",
        out_shape=(jax.ShapeDtypeStruct(direction.shape, F32), jax.ShapeDtypeStruct((1, T), F32), jax.ShapeDtypeStruct((1, T), F32)),
        in_specs=[anywhere] * 5,
        out_specs=(anywhere,) * 3,
        scratch_shapes=[
            v(512, 256), v(1024, 256), v(1024, 512), v(512, T), v(512, T), v(512, T),
            v(4, 256, T), v(4, 256, T), v(4, 256, T), v(4, 3, H, T), v(4, 4, H, T), v(4, 512, T),
            v(4, 512, T), v(4, 3, H, T), v(4, 5, H, T), v(4, 2, H // 2, T), v(4, 2, H // 2, T), v(4, 256, T),
            h(512, 1024), h(512, 1024), h(1024, 512), h(1024, 512), h(512, 1024), h(512, 1024),
            v(32, 1, 3 * T), v(32, 1, T), v(2, 1, T),
            dma((2, 9)), dma((4, 15)), dma((2,)), dma((2,)), dma((9,)),
        ],
        compiler_params=pltpu.CompilerParams(collective_id=0, has_side_effects=True, vmem_limit_bytes=60 * 2**20),
    )(points, centers, factor, residual, direction)
    new_solution = solution_ + step_size * direction
    new_residual = residual - step_size * (image + ridge_weight * direction)
    return new_solution, new_residual, new_residual + ratio * direction


def solution(mesh):
    return jax.shard_map(
        body,
        mesh=mesh,
        in_specs=(
            P("rows", None),
            P("cols", None),
            P("cols", "rows"),
            P("rows", None),
            P("rows", None),
            P("rows", None),
        ),
        out_specs=(P("rows", None), P("rows", None), P("rows", None)),
        check_vma=False,
    )
```

```python
import jax
import jax.numpy as jnp
from jax import lax
from jax.experimental import pallas as pl
from jax.experimental.pallas import tpu as pltpu
from jax.sharding import PartitionSpec as P

ridge_weight = 0.02
MESH = pl.DeviceIdType.MESH
F32, BF16 = jnp.float32, jnp.bfloat16
T = 128
W = 64
Q = 128
H = 64


def split(a):
    high = a.astype(BF16)
    return high, (a - high.astype(F32)).astype(BF16)


def swap(a):
    return pltpu.roll(a, W, 1)


def first_lanes(rows):
    return lax.broadcasted_iota(jnp.int32, (rows, T), 1) < W


def pack(full, chain):
    top, bottom = full[:H], full[H:]
    if chain == 0:
        return jnp.where(first_lanes(H), top, swap(bottom))
    return jnp.where(first_lanes(H), swap(top), bottom)


def unpack(a, b):
    m = first_lanes(H)
    return jnp.concatenate([jnp.where(m, a, swap(b)), jnp.where(m, swap(a), b)], axis=0)


def fold(both):
    total = both + swap(both)
    return jnp.where(first_lanes(H), total[:H], total[H:])


def operand(packed):
    high = packed.astype(BF16).astype(F32)
    low = packed - high
    m = first_lanes(H)
    return jnp.concatenate([jnp.where(m, high, swap(low)), jnp.where(m, swap(high), low)], axis=0).astype(BF16)


def dot(a, b):
    return jnp.dot(a, b, preferred_element_type=F32)


def across(a, b):
    return lax.dot_general(
        a, b, (((1,), (1,)), ((), ())), precision=lax.Precision.HIGHEST, preferred_element_type=F32
    )


def rows_of(start, size):
    return pl.ds(pl.multiple_of(start, size), size)


def kernel(
    points_, centers_, factor_, residual_, direction_,
    image_, step_out, ratio_out,
    points, centers, factor, residual, direction, image,
    away, own, core_in, a_in, b_in, full_c,
    part, x_in, zh_out, zh_in1, zh_in2, full_r,
    kh, kl, kth, ktl, rth, rtl,
    small_a, small_b, small_x, line,
    send, recv, small_send, small_recv, local,
):
    r, c = lax.axis_index("rows"), lax.axis_index("cols")
    y, k = lax.div(r, 8), lax.rem(r, 2)
    zl = lax.rem(lax.div(r, 2), 4)
    x, zh = lax.div(c, 4), lax.rem(c, 4)

    def turn(v, j):
        return v if isinstance(j, int) and j == 0 else lax.rem(v + j, 4)

    def at(y_=None, zl_=None, k_=None, x_=None, zh_=None):
        pick = lambda new, old: old if new is None else new
        return (pick(y_, y) * 8 + pick(zl_, zl) * 2 + pick(k_, k), pick(x_, x) * 4 + pick(zh_, zh))

    sibling = at(k_=1 - k)
    ys = [at(y_=turn(y, j)) for j in (1, 2, 3)]
    zls = [at(zl_=turn(zl, j)) for j in (1, 2, 3)]
    xs = [at(x_=turn(x, j)) for j in (1, 2, 3)]
    zh_a = at(zh_=zh + 1 - 2 * lax.rem(zh, 2))
    zh_b = at(zh_=turn(zh, 3 - 2 * lax.rem(zh, 2)))
    column = [
        at(turn(y, i), turn(zl, j), 1 - k if e else k) for i in (2, 1, 3, 0) for j in (2, 1, 3, 0) for e in (1, 0)
    ][:-1]

    here_half, there_half = rows_of(k * 512, 512), rows_of((1 - k) * 512, 512)
    loads = [
        pltpu.make_async_copy(a, b, local.at[i])
        for i, (a, b) in enumerate(
            [
                (direction_, direction),
                (factor_.at[there_half], factor.at[there_half]),
                (factor_.at[here_half], factor.at[here_half]),
                (centers_, centers),
                (points_, points),
                (residual_, residual),
            ]
        )
    ]
    loads[0].start()
    loads[1].start()

    peers = [zh_a, zh_b] + column + xs
    barrier = pltpu.get_barrier_semaphore()
    for p in peers:
        pl.semaphore_signal(barrier, inc=1, device_id=p, device_id_type=MESH)

    for load in loads[2:]:
        load.start()

    def copy(src, dst, s, d, device):
        return pltpu.make_async_remote_copy(
            src_ref=src, dst_ref=dst, send_sem=s, recv_sem=d, device_id=device, device_id_type=MESH
        )

    small = [small_a, small_b]

    def push(src, dst, s, phase, d, device):
        copy(src, dst, send.at[s % 2, phase], recv.at[s, d], device).start()

    def arrived(like, s, d):
        copy(like, like, send.at[s % 2, 0], recv.at[s, d], sibling).wait_recv()

    def sent(s, phase):
        like = {0: away, 4: away, 6: zh_in1, 7: zh_in2}.get(phase, a_in).at[s]
        copy(like, like, send.at[s % 2, phase], recv.at[s, 0], sibling).wait_send()

    def small_start(n, value):
        lines = small[n]
        lines[r] = value
        for device in column:
            copy(lines.at[r], lines.at[r], small_send.at[n], small_recv.at[n], device).start()

    def small_end(n):
        like = small[n].at[pl.ds(0, 31)]
        copy(like, like, small_send.at[n], small_recv.at[n], sibling).wait()
        return jnp.sum(small[n][...], axis=0)

    def send_away(s):
        if s > 1:
            sent(s, 0)
        for q in range(4):
            rows = pl.ds(q * H, H)
            push(away.at[s, rows], core_in.at[s, rows], s, 0, 0, sibling)

    def chain(p, n, high, low):
        s = 2 * n + p
        (a, a_devices), (b, b_devices) = [((y, ys), (zl, zls)), ((zl, zls), (y, ys))][p]

        def again(*phases):
            for phase in phases if n else ():
                sent(s, phase)

        yield
        again(1)
        arrived(core_in.at[s], s, 0)
        own[s] = own[s] + core_in[s]
        for j in (2, 1, 3):
            push(own.at[s, rows_of((a + j) % 4 * H, H)], a_in.at[s, j - 1], s, 1, 1, a_devices[j - 1])
        again(2)
        yield
        mine = rows_of(a * H, H)
        arrived(a_in.at[s], s, 1)
        b_in[s, b] = (own[s, mine] + a_in[s, 0]) + (a_in[s, 1] + a_in[s, 2])
        for j in (2, 1, 3):
            push(b_in.at[s, b], b_in.at[s, b], s, 2, 2, b_devices[j - 1])
        again(3, 4)
        yield
        arrived(a_in.at[s], s, 2)
        here = rows_of(k * 256 + a * H, H)
        full_c[s, here] = (b_in[s, 0] + b_in[s, 1]) + (b_in[s, 2] + b_in[s, 3])
        for j in (2, 1, 3):
            push(full_c.at[s, here], full_c.at[s, here], s, 3, 3 + j - 1, a_devices[j - 1])
        push(full_c.at[s, here], full_c.at[s, here], s, 4, 6, sibling)
        yield
        for j in (1, 3, 2):
            there = rows_of(k * 256 + (a + 4 - j) % 4 * H, H)
            arrived(full_c.at[s, there], s, 3 + j - 1)
            push(full_c.at[s, there], full_c.at[s, there], s, 4, 6, sibling)
        mine, his = rows_of(k * 512, 512), rows_of((1 - k) * 512, 512)

        def half(base):
            return jnp.concatenate([operand(full_c[s, rows_of(base * 256 + q * H, H)]) for q in range(4)], axis=0)

        term = half(k)
        for q in range(4):
            rows = pl.ds(q * Q, Q)
            part[s, rows] = dot(high[rows, mine], term) + dot(low[rows, mine], term)
        again(5)
        yield
        arrived(full_c.at[s, rows_of((1 - k) * 256, 256)], s, 6)
        term = half(1 - k)
        slots = [zh_out.at[s, 0], zh_out.at[s, 2], zh_out.at[s, 3], zh_out.at[s, 4]]
        for j in range(4):
            rows = rows_of((x + j) % 4 * Q, Q)
            slots[j][...] = fold(part[s, rows] + (dot(high[rows, his], term) + dot(low[rows, his], term)))
        for j in (2, 1, 3):
            push(slots[j], x_in.at[s, j - 1], s, 5, 7, xs[j - 1])
        again(6, 7)
        yield
        arrived(x_in.at[s], s, 7)
        zh_out[s, 0] = (zh_out[s, 0] + x_in[s, 0]) + (x_in[s, 1] + x_in[s, 2])
        first, second = pl.ds(0, H // 2), pl.ds(H // 2, H // 2)
        push(zh_out.at[s, 0, first], zh_in1.at[s, 0], s, 6, 8, zh_a)
        push(zh_out.at[s, 0, second], zh_in1.at[s, 1], s, 6, 9, zh_b)
        yield
        arrived(zh_in1.at[s, 0], s, 8)
        zh_out[s, 1, first] = zh_out[s, 0, first] + zh_in1[s, 0]
        push(zh_out.at[s, 1, first], zh_in2.at[s, 0], s, 7, 10, zh_b)
        arrived(zh_in1.at[s, 1], s, 9)
        zh_out[s, 1, second] = zh_out[s, 0, second] + zh_in1[s, 1]
        push(zh_out.at[s, 1, second], zh_in2.at[s, 1], s, 7, 10, zh_a)
        again(8)
        yield
        here = rows_of(x * H, H)
        arrived(zh_in2.at[s], s, 10)
        full_r[s, here] = zh_out[s, 1] + zh_in2[s].reshape(H, T)
        if s == 3:
            yield
        for j in (2, 1, 3):
            push(full_r.at[s, here], full_r.at[s, here], s, 8, 11, xs[j - 1])
        yield
        arrived(x_in.at[s], s, 11)

    def back_terms(p):
        s = 2 + p
        b = jnp.concatenate([operand(full_r[p, q * H : (q + 1) * H]) for q in range(4)], axis=0)
        for q in range(4):
            rows = rows_of((1 - k) * 512 + q * Q, Q)
            away[s, q * H : (q + 1) * H] = fold(dot(kth[rows, :], b) + dot(ktl[rows, :], b))
        send_away(s)
        for q in range(4):
            rows = rows_of(k * 512 + q * Q, Q)
            own[s, q * H : (q + 1) * H] = fold(dot(kth[rows, :], b) + dot(ktl[rows, :], b))

    def whole(p):
        yield from chain(p, 0, kh, kl)
        back_terms(p)
        yield from chain(p, 1, rth, rtl)

    def kernel_block(e):
        def run():
            if e == 0:
                loads[3].wait()
                loads[4].wait()
            cols = slice(e * 256, (e + 1) * 256)
            a, b = points[...], centers[cols, :]
            a_sq = jnp.sum(a * a, axis=1, keepdims=True)
            b_sq = across(jnp.ones((8, b.shape[1]), F32), b * b)[0:1]
            block = jnp.exp(-0.5 * ((a_sq + b_sq) - 2.0 * across(a, b)))
            kh[:, cols], kl[:, cols] = split(block)
            kth[cols, :], ktl[cols, :] = split(block.T)

        return run

    def factor_block(e):
        def run():
            cols = slice(e * 256, (e + 1) * 256)
            rth[:, cols], rtl[:, cols] = split(factor[cols, :].T)

        return run

    def norm(a):
        return jnp.sum(a * a, axis=0, keepdims=True)

    def first_norms():
        loads[5].wait()
        squares = [norm(full_r[p]) for p in (0, 1)]
        squares = [a + swap(a) for a in squares]
        predicted = jnp.where(first_lanes(1), squares[0], squares[1])
        small_start(0, jnp.concatenate([norm(residual[...]), norm(direction[...]), predicted], axis=1))

    loads[0].wait()
    pair = jnp.concatenate(split(direction[...]), axis=1)

    def mapped(base, target):
        for q in range(4):
            high, low = split(factor[rows_of(base * 512 + q * Q, Q), :])
            both = dot(high, pair) + dot(low, pair)
            both = both[:, :T] + both[:, T:]
            for p in (0, 1):
                target[p, q * H : (q + 1) * H] = pack(both, p)

    loads[1].wait()
    mapped(1 - k, away)
    pl.semaphore_wait(barrier, len(peers))
    for p in (0, 1):
        send_away(p)
    loads[2].wait()
    mapped(k, own)

    chains = [whole(0), whole(1)]
    extra = {
        1: [kernel_block(0), kernel_block(1)],
        2: [kernel_block(2), kernel_block(3)],
        6: [factor_block(0), factor_block(1)],
        7: [factor_block(2), factor_block(3)],
        10: [first_norms],
    }
    for step in range(18):
        for p in (1, 0) if step in (3, 12) else (0, 1):
            next(chains[p])
        for run in extra.get(step, []):
            run()

    sums = small_end(0)
    norm_now = sums[:, :T]
    step_size = norm_now / (sums[:, 2 * T :] + ridge_weight * sums[:, T : 2 * T])
    quarter, packed = rows_of(x * Q, Q), rows_of(x * H, H)
    fresh = residual[quarter, :] - step_size * (
        unpack(full_r[2, packed], full_r[3, packed]) + ridge_weight * direction[quarter, :]
    )
    small_x[x] = norm(fresh)
    for device in xs:
        copy(small_x.at[x], small_x.at[x], small_send.at[2], small_recv.at[2], device).start()
    next(chains[1])
    line[0] = step_size
    outs = [pltpu.make_async_copy(line.at[0], step_out, local.at[6])]
    outs[0].start()
    like = small_x.at[pl.ds(0, 3)]
    copy(like, like, small_send.at[2], small_recv.at[2], sibling).wait()
    small_start(1, jnp.sum(small_x[...], axis=0))
    for p in (0, 1):
        for unused in chains[p]:
            pass
    for q in range(4):
        packed = pl.ds(q * H, H)
        image[q * Q : (q + 1) * Q] = unpack(full_r[2, packed], full_r[3, packed])
    outs.append(pltpu.make_async_copy(image, image_, local.at[7]))
    outs[1].start()
    for p in (0, 1):
        for phase in range(9):
            sent(2 + p, phase)
    for out in outs:
        out.wait()
    line[1] = small_end(1) / norm_now
    last = pltpu.make_async_copy(line.at[1], ratio_out, local.at[8])
    last.start()
    last.wait()


def body(points, centers, factor, solution_, residual, direction):
    anywhere = pl.BlockSpec(memory_space=pl.ANY)
    dma = pltpu.SemaphoreType.DMA
    v = lambda *shape: pltpu.VMEM(shape, F32)
    h = lambda *shape: pltpu.VMEM(shape, BF16)
    image, step_size, ratio = pl.pallas_call(
        kernel,
        name="cg_iteration",
        out_shape=(jax.ShapeDtypeStruct(direction.shape, F32), jax.ShapeDtypeStruct((1, T), F32), jax.ShapeDtypeStruct((1, T), F32)),
        in_specs=[anywhere] * 5,
        out_specs=(anywhere,) * 3,
        scratch_shapes=[
            v(512, 256), v(1024, 256), v(1024, 512), v(512, T), v(512, T), v(512, T),
            v(4, 256, T), v(4, 256, T), v(4, 256, T), v(4, 3, H, T), v(4, 4, H, T), v(4, 512, T),
            v(4, 512, T), v(4, 3, H, T), v(4, 5, H, T), v(4, 2, H // 2, T), v(4, 2, H // 2, T), v(4, 256, T),
            h(512, 1024), h(512, 1024), h(1024, 512), h(1024, 512), h(512, 1024), h(512, 1024),
            v(32, 1, 3 * T), v(32, 1, T), v(4, 1, T), v(2, 1, T),
            dma((2, 9)), dma((4, 12)), dma((3,)), dma((3,)), dma((9,)),
        ],
        compiler_params=pltpu.CompilerParams(collective_id=0, has_side_effects=True, vmem_limit_bytes=60 * 2**20),
    )(points, centers, factor, residual, direction)
    new_solution = solution_ + step_size * direction
    new_residual = residual - step_size * (image + ridge_weight * direction)
    return new_solution, new_residual, new_residual + ratio * direction


def solution(mesh):
    return jax.shard_map(
        body,
        mesh=mesh,
        in_specs=(
            P("rows", None),
            P("cols", None),
            P("cols", "rows"),
            P("rows", None),
            P("rows", None),
            P("rows", None),
        ),
        out_specs=(P("rows", None), P("rows", None), P("rows", None)),
        check_vma=False,
    )
```

```python
import jax
import jax.numpy as jnp
from jax import lax
from jax.experimental import pallas as pl
from jax.experimental.pallas import tpu as pltpu
from jax.sharding import PartitionSpec as P

ridge_weight = 0.02
MESH = pl.DeviceIdType.MESH
F32, BF16 = jnp.float32, jnp.bfloat16
T = 128
W = 64
Q = 128
H = 64


def split(a):
    high = a.astype(BF16)
    return high, (a - high.astype(F32)).astype(BF16)


def swap(a):
    return pltpu.roll(a, W, 1)


def first_lanes(rows):
    return lax.broadcasted_iota(jnp.int32, (rows, T), 1) < W


def pack(full, chain):
    top, bottom = full[:H], full[H:]
    if chain == 0:
        return jnp.where(first_lanes(H), top, swap(bottom))
    return jnp.where(first_lanes(H), swap(top), bottom)


def unpack(a, b):
    m = first_lanes(H)
    return jnp.concatenate([jnp.where(m, a, swap(b)), jnp.where(m, swap(a), b)], axis=0)


def fold(both):
    total = both + swap(both)
    return jnp.where(first_lanes(H), total[:H], total[H:])


def operand(packed):
    high = packed.astype(BF16).astype(F32)
    low = packed - high
    m = first_lanes(H)
    return jnp.concatenate([jnp.where(m, high, swap(low)), jnp.where(m, swap(high), low)], axis=0).astype(BF16)


def dot(a, b):
    return jnp.dot(a, b, preferred_element_type=F32)


def across(a, b):
    return lax.dot_general(
        a, b, (((1,), (1,)), ((), ())), precision=lax.Precision.HIGHEST, preferred_element_type=F32
    )


def rows_of(start, size):
    return pl.ds(pl.multiple_of(start, size), size)


def kernel(
    points_, centers_, factor_, residual_, direction_,
    image_, step_out, ratio_out,
    points, centers, factor, residual, direction, image,
    away, own, core_in, a_in, b_in, full_c,
    part, x_in, zh_out, zh_in1, zh_in2, full_r,
    kh, kl, kth, ktl, rth, rtl,
    small_a, small_b, small_x, line,
    send, recv, small_send, small_recv, local,
):
    r, c = lax.axis_index("rows"), lax.axis_index("cols")
    y, k = lax.div(r, 8), lax.rem(r, 2)
    zl = lax.rem(lax.div(r, 2), 4)
    x, zh = lax.div(c, 4), lax.rem(c, 4)

    def turn(v, j):
        return v if isinstance(j, int) and j == 0 else lax.rem(v + j, 4)

    def at(y_=None, zl_=None, k_=None, x_=None, zh_=None):
        pick = lambda new, old: old if new is None else new
        return (pick(y_, y) * 8 + pick(zl_, zl) * 2 + pick(k_, k), pick(x_, x) * 4 + pick(zh_, zh))

    sibling = at(k_=1 - k)
    ys = [at(y_=turn(y, j)) for j in (1, 2, 3)]
    zls = [at(zl_=turn(zl, j)) for j in (1, 2, 3)]
    xs = [at(x_=turn(x, j)) for j in (1, 2, 3)]
    zh_a = at(zh_=zh + 1 - 2 * lax.rem(zh, 2))
    zh_b = at(zh_=turn(zh, 3 - 2 * lax.rem(zh, 2)))
    column = [
        at(turn(y, i), turn(zl, j), 1 - k if e else k) for i in (2, 1, 3, 0) for j in (2, 1, 3, 0) for e in (1, 0)
    ][:-1]

    here_half, there_half = rows_of(k * 512, 512), rows_of((1 - k) * 512, 512)
    loads = [
        pltpu.make_async_copy(a, b, local.at[i])
        for i, (a, b) in enumerate(
            [
                (direction_, direction),
                (factor_.at[there_half], factor.at[there_half]),
                (factor_.at[here_half], factor.at[here_half]),
                (centers_, centers),
                (points_, points),
                (residual_, residual),
            ]
        )
    ]
    loads[0].start()
    loads[1].start()

    peers = [zh_a, zh_b] + zls + ys + xs + [sibling]
    barrier = pltpu.get_barrier_semaphore()
    for p in peers:
        pl.semaphore_signal(barrier, inc=1, device_id=p, device_id_type=MESH)

    for load in loads[2:]:
        load.start()

    def copy(src, dst, s, d, device):
        return pltpu.make_async_remote_copy(
            src_ref=src, dst_ref=dst, send_sem=s, recv_sem=d, device_id=device, device_id_type=MESH
        )

    small = [small_a, small_b]

    def push(src, dst, s, phase, d, device):
        copy(src, dst, send.at[s % 2, phase], recv.at[s, d], device).start()

    def arrived(like, s, d):
        copy(like, like, send.at[s % 2, 0], recv.at[s, d], sibling).wait_recv()

    def sent(s, phase):
        like = {0: away, 4: away, 6: zh_in1, 7: zh_in2}.get(phase, a_in).at[s]
        copy(like, like, send.at[s % 2, phase], recv.at[s, 0], sibling).wait_send()

    def small_start(n, value):
        lines = small[n]
        lines[r] = value
        for device in column:
            copy(lines.at[r], lines.at[r], small_send.at[n], small_recv.at[n], device).start()

    def small_end(n):
        like = small[n].at[pl.ds(0, 31)]
        copy(like, like, small_send.at[n], small_recv.at[n], sibling).wait()
        return jnp.sum(small[n][...], axis=0)

    def send_away(s):
        if s > 1:
            sent(s, 0)
        for q in range(4):
            rows = pl.ds(q * H, H)
            push(away.at[s, rows], core_in.at[s, rows], s, 0, 0, sibling)

    def chain(p, n, high, low):
        s = 2 * n + p
        (a, a_devices), (b, b_devices) = [((y, ys), (zl, zls)), ((zl, zls), (y, ys))][p]

        def again(*phases):
            for phase in phases if n else ():
                sent(s, phase)

        yield
        again(1)
        arrived(core_in.at[s], s, 0)
        own[s] = own[s] + core_in[s]
        for j in (2, 1, 3):
            push(own.at[s, rows_of((a + j) % 4 * H, H)], a_in.at[s, j - 1], s, 1, 1, a_devices[j - 1])
        again(2)
        yield
        mine = rows_of(a * H, H)
        arrived(a_in.at[s], s, 1)
        b_in[s, b] = (own[s, mine] + a_in[s, 0]) + (a_in[s, 1] + a_in[s, 2])
        for j in (2, 1, 3):
            push(b_in.at[s, b], b_in.at[s, b], s, 2, 2, b_devices[j - 1])
        again(3, 4)
        yield
        arrived(a_in.at[s], s, 2)
        here = rows_of(k * 256 + a * H, H)
        full_c[s, here] = (b_in[s, 0] + b_in[s, 1]) + (b_in[s, 2] + b_in[s, 3])
        for j in (2, 1, 3):
            push(full_c.at[s, here], full_c.at[s, here], s, 3, 3 + j - 1, a_devices[j - 1])
        push(full_c.at[s, here], full_c.at[s, here], s, 4, 6, sibling)
        yield
        for j in (1, 3, 2):
            there = rows_of(k * 256 + (a + 4 - j) % 4 * H, H)
            arrived(full_c.at[s, there], s, 3 + j - 1)
            push(full_c.at[s, there], full_c.at[s, there], s, 4, 6, sibling)
        mine, his = rows_of(k * 512, 512), rows_of((1 - k) * 512, 512)

        def half(base):
            return jnp.concatenate([operand(full_c[s, rows_of(base * 256 + q * H, H)]) for q in range(4)], axis=0)

        term = half(k)
        for q in range(4):
            rows = pl.ds(q * Q, Q)
            part[s, rows] = dot(high[rows, mine], term) + dot(low[rows, mine], term)
        again(5)
        yield
        arrived(full_c.at[s, rows_of((1 - k) * 256, 256)], s, 6)
        term = half(1 - k)
        slots = [zh_out.at[s, 0], zh_out.at[s, 2], zh_out.at[s, 3], zh_out.at[s, 4]]
        for j in range(4):
            rows = rows_of((x + j) % 4 * Q, Q)
            slots[j][...] = fold(part[s, rows] + (dot(high[rows, his], term) + dot(low[rows, his], term)))
        for j in (2, 1, 3):
            push(slots[j], x_in.at[s, j - 1], s, 5, 7, xs[j - 1])
        again(6, 7)
        yield
        arrived(x_in.at[s], s, 7)
        zh_out[s, 0] = (zh_out[s, 0] + x_in[s, 0]) + (x_in[s, 1] + x_in[s, 2])
        first, second = pl.ds(0, H // 2), pl.ds(H // 2, H // 2)
        push(zh_out.at[s, 0, first], zh_in1.at[s, 0], s, 6, 8, zh_a)
        push(zh_out.at[s, 0, second], zh_in1.at[s, 1], s, 6, 9, zh_b)
        yield
        arrived(zh_in1.at[s, 0], s, 8)
        zh_out[s, 1, first] = zh_out[s, 0, first] + zh_in1[s, 0]
        push(zh_out.at[s, 1, first], zh_in2.at[s, 0], s, 7, 10, zh_b)
        arrived(zh_in1.at[s, 1], s, 9)
        zh_out[s, 1, second] = zh_out[s, 0, second] + zh_in1[s, 1]
        push(zh_out.at[s, 1, second], zh_in2.at[s, 1], s, 7, 10, zh_a)
        again(8)
        yield
        here = rows_of(x * H, H)
        arrived(zh_in2.at[s], s, 10)
        full_r[s, here] = zh_out[s, 1] + zh_in2[s].reshape(H, T)
        if s == 3:
            yield
        for j in (2, 1, 3):
            push(full_r.at[s, here], full_r.at[s, here], s, 8, 11, xs[j - 1])
        yield
        arrived(x_in.at[s], s, 11)

    def back_terms(p):
        s = 2 + p
        b = jnp.concatenate([operand(full_r[p, q * H : (q + 1) * H]) for q in range(4)], axis=0)
        for q in range(4):
            rows = rows_of((1 - k) * 512 + q * Q, Q)
            away[s, q * H : (q + 1) * H] = fold(dot(kth[rows, :], b) + dot(ktl[rows, :], b))
        send_away(s)
        for q in range(4):
            rows = rows_of(k * 512 + q * Q, Q)
            own[s, q * H : (q + 1) * H] = fold(dot(kth[rows, :], b) + dot(ktl[rows, :], b))

    def whole(p):
        yield from chain(p, 0, kh, kl)
        back_terms(p)
        yield from chain(p, 1, rth, rtl)

    def kernel_block(e):
        def run():
            if e == 0:
                loads[3].wait()
                loads[4].wait()
            cols = slice(e * 256, (e + 1) * 256)
            a, b = points[...], centers[cols, :]
            a_sq = jnp.sum(a * a, axis=1, keepdims=True)
            b_sq = across(jnp.ones((8, b.shape[1]), F32), b * b)[0:1]
            block = jnp.exp(-0.5 * ((a_sq + b_sq) - 2.0 * across(a, b)))
            kh[:, cols], kl[:, cols] = split(block)
            kth[cols, :], ktl[cols, :] = split(block.T)

        return run

    def factor_block(e):
        def run():
            cols = slice(e * 256, (e + 1) * 256)
            rth[:, cols], rtl[:, cols] = split(factor[cols, :].T)

        return run

    def norm(a):
        return jnp.sum(a * a, axis=0, keepdims=True)

    def first_norms():
        loads[5].wait()
        squares = [norm(full_r[p]) for p in (0, 1)]
        squares = [a + swap(a) for a in squares]
        predicted = jnp.where(first_lanes(1), squares[0], squares[1])
        small_start(0, jnp.concatenate([norm(residual[...]), norm(direction[...]), predicted], axis=1))

    loads[0].wait()
    pair = jnp.concatenate(split(direction[...]), axis=1)

    def mapped(base, target):
        for q in range(4):
            high, low = split(factor[rows_of(base * 512 + q * Q, Q), :])
            both = dot(high, pair) + dot(low, pair)
            both = both[:, :T] + both[:, T:]
            for p in (0, 1):
                target[p, q * H : (q + 1) * H] = pack(both, p)

    loads[1].wait()
    mapped(1 - k, away)
    pl.semaphore_wait(barrier, len(peers))
    for p in (0, 1):
        send_away(p)
    loads[2].wait()
    mapped(k, own)

    chains = [whole(0), whole(1)]
    extra = {
        1: [kernel_block(0), kernel_block(1)],
        2: [kernel_block(2), kernel_block(3)],
        6: [factor_block(0), factor_block(1)],
        7: [factor_block(2), factor_block(3)],
        10: [first_norms],
    }
    for step in range(18):
        for p in (1, 0) if step in (3, 12) else (0, 1):
            next(chains[p])
        for run in extra.get(step, []):
            run()

    sums = small_end(0)
    norm_now = sums[:, :T]
    step_size = norm_now / (sums[:, 2 * T :] + ridge_weight * sums[:, T : 2 * T])
    quarter, packed = rows_of(x * Q, Q), rows_of(x * H, H)
    fresh = residual[quarter, :] - step_size * (
        unpack(full_r[2, packed], full_r[3, packed]) + ridge_weight * direction[quarter, :]
    )
    small_x[x] = norm(fresh)
    for device in xs:
        copy(small_x.at[x], small_x.at[x], small_send.at[2], small_recv.at[2], device).start()
    next(chains[1])
    line[0] = step_size
    outs = [pltpu.make_async_copy(line.at[0], step_out, local.at[6])]
    outs[0].start()
    like = small_x.at[pl.ds(0, 3)]
    copy(like, like, small_send.at[2], small_recv.at[2], sibling).wait()
    small_start(1, jnp.sum(small_x[...], axis=0))
    for p in (0, 1):
        for unused in chains[p]:
            pass
    for q in range(4):
        packed = pl.ds(q * H, H)
        image[q * Q : (q + 1) * Q] = unpack(full_r[2, packed], full_r[3, packed])
    outs.append(pltpu.make_async_copy(image, image_, local.at[7]))
    outs[1].start()
    for p in (0, 1):
        for phase in range(9):
            sent(2 + p, phase)
    for out in outs:
        out.wait()
    line[1] = small_end(1) / norm_now
    last = pltpu.make_async_copy(line.at[1], ratio_out, local.at[8])
    last.start()
    last.wait()


def body(points, centers, factor, solution_, residual, direction):
    anywhere = pl.BlockSpec(memory_space=pl.ANY)
    dma = pltpu.SemaphoreType.DMA
    v = lambda *shape: pltpu.VMEM(shape, F32)
    h = lambda *shape: pltpu.VMEM(shape, BF16)
    image, step_size, ratio = pl.pallas_call(
        kernel,
        name="cg_iteration",
        out_shape=(jax.ShapeDtypeStruct(direction.shape, F32), jax.ShapeDtypeStruct((1, T), F32), jax.ShapeDtypeStruct((1, T), F32)),
        in_specs=[anywhere] * 5,
        out_specs=(anywhere,) * 3,
        scratch_shapes=[
            v(512, 256), v(1024, 256), v(1024, 512), v(512, T), v(512, T), v(512, T),
            v(4, 256, T), v(4, 256, T), v(4, 256, T), v(4, 3, H, T), v(4, 4, H, T), v(4, 512, T),
            v(4, 512, T), v(4, 3, H, T), v(4, 5, H, T), v(4, 2, H // 2, T), v(4, 2, H // 2, T), v(4, 256, T),
            h(512, 1024), h(512, 1024), h(1024, 512), h(1024, 512), h(512, 1024), h(512, 1024),
            v(32, 1, 3 * T), v(32, 1, T), v(4, 1, T), v(2, 1, T),
            dma((2, 9)), dma((4, 12)), dma((3,)), dma((3,)), dma((9,)),
        ],
        compiler_params=pltpu.CompilerParams(collective_id=0, has_side_effects=True, vmem_limit_bytes=60 * 2**20),
    )(points, centers, factor, residual, direction)
    new_solution = solution_ + step_size * direction
    new_residual = residual - step_size * (image + ridge_weight * direction)
    return new_solution, new_residual, new_residual + ratio * direction


def solution(mesh):
    return jax.shard_map(
        body,
        mesh=mesh,
        in_specs=(
            P("rows", None),
            P("cols", None),
            P("cols", "rows"),
            P("rows", None),
            P("rows", None),
            P("rows", None),
        ),
        out_specs=(P("rows", None), P("rows", None), P("rows", None)),
        check_vma=False,
    )
```

```python
import jax
import jax.numpy as jnp
from jax import lax
from jax.experimental import pallas as pl
from jax.experimental.pallas import tpu as pltpu
from jax.sharding import PartitionSpec as P

ridge_weight = 0.02
MESH = pl.DeviceIdType.MESH
F32, BF16 = jnp.float32, jnp.bfloat16
T = 128
W = 64
Q = 128
H = 64


def split(a):
    high = a.astype(BF16)
    return high, (a - high.astype(F32)).astype(BF16)


def swap(a):
    return pltpu.roll(a, W, 1)


def first_lanes(rows):
    return lax.broadcasted_iota(jnp.int32, (rows, T), 1) < W


def pack(full, chain):
    top, bottom = full[:H], full[H:]
    if chain == 0:
        return jnp.where(first_lanes(H), top, swap(bottom))
    return jnp.where(first_lanes(H), swap(top), bottom)


def unpack(a, b):
    m = first_lanes(H)
    return jnp.concatenate([jnp.where(m, a, swap(b)), jnp.where(m, swap(a), b)], axis=0)


def fold(both):
    total = both + swap(both)
    return jnp.where(first_lanes(H), total[:H], total[H:])


def operand(packed):
    high = packed.astype(BF16).astype(F32)
    low = packed - high
    m = first_lanes(H)
    return jnp.concatenate([jnp.where(m, high, swap(low)), jnp.where(m, swap(high), low)], axis=0).astype(BF16)


def dot(a, b):
    return jnp.dot(a, b, preferred_element_type=F32)


def across(a, b):
    return lax.dot_general(
        a, b, (((1,), (1,)), ((), ())), precision=lax.Precision.HIGHEST, preferred_element_type=F32
    )


def rows_of(start, size):
    return pl.ds(pl.multiple_of(start, size), size)


def kernel(
    points_, centers_, factor_, residual_, direction_,
    image_, step_out, ratio_out,
    points, centers, factor, residual, direction, image,
    away, own, core_in, a_in, b_in, full_c,
    part, x_in, zh_out, zh_in1, zh_in2, full_r,
    kh, kl, kth, ktl, rth, rtl,
    small_a, small_b, small_x, line,
    send, recv, small_send, small_recv, local,
):
    r, c = lax.axis_index("rows"), lax.axis_index("cols")
    y, k = lax.div(r, 8), lax.rem(r, 2)
    zl = lax.rem(lax.div(r, 2), 4)
    x, zh = lax.div(c, 4), lax.rem(c, 4)

    def turn(v, j):
        return v if isinstance(j, int) and j == 0 else lax.rem(v + j, 4)

    def at(y_=None, zl_=None, k_=None, x_=None, zh_=None):
        pick = lambda new, old: old if new is None else new
        return (pick(y_, y) * 8 + pick(zl_, zl) * 2 + pick(k_, k), pick(x_, x) * 4 + pick(zh_, zh))

    sibling = at(k_=1 - k)
    ys = [at(y_=turn(y, j)) for j in (1, 2, 3)]
    zls = [at(zl_=turn(zl, j)) for j in (1, 2, 3)]
    xs = [at(x_=turn(x, j)) for j in (1, 2, 3)]
    zh_a = at(zh_=zh + 1 - 2 * lax.rem(zh, 2))
    zh_b = at(zh_=turn(zh, 3 - 2 * lax.rem(zh, 2)))
    column = [
        at(turn(y, i), turn(zl, j), 1 - k if e else k) for i in (2, 1, 3, 0) for j in (2, 1, 3, 0) for e in (1, 0)
    ][:-1]

    here_half, there_half = rows_of(k * 512, 512), rows_of((1 - k) * 512, 512)
    loads = [
        pltpu.make_async_copy(a, b, local.at[i])
        for i, (a, b) in enumerate(
            [
                (direction_, direction),
                (factor_.at[there_half], factor.at[there_half]),
                (factor_.at[here_half], factor.at[here_half]),
                (centers_, centers),
                (points_, points),
                (residual_, residual),
            ]
        )
    ]
    loads[0].start()
    loads[1].start()

    peers = [zh_a, zh_b] + zls + ys + xs + [sibling]
    barrier = pltpu.get_barrier_semaphore()
    for p in peers:
        pl.semaphore_signal(barrier, inc=1, device_id=p, device_id_type=MESH)

    for load in loads[2:]:
        load.start()

    def copy(src, dst, s, d, device):
        return pltpu.make_async_remote_copy(
            src_ref=src, dst_ref=dst, send_sem=s, recv_sem=d, device_id=device, device_id_type=MESH
        )

    small = [small_a, small_b]

    def push(src, dst, s, phase, d, device):
        copy(src, dst, send.at[s % 2, phase], recv.at[s, d], device).start()

    def arrived(like, s, d):
        copy(like, like, send.at[s % 2, 0], recv.at[s, d], sibling).wait_recv()

    def sent(s, phase):
        like = {0: away, 4: away, 6: zh_in1, 7: zh_in2}.get(phase, a_in).at[s]
        copy(like, like, send.at[s % 2, phase], recv.at[s, 0], sibling).wait_send()

    def small_start(n, value):
        lines = small[n]
        lines[r] = value
        for device in column:
            copy(lines.at[r], lines.at[r], small_send.at[n], small_recv.at[n], device).start()

    def small_end(n):
        like = small[n].at[pl.ds(0, 31)]
        copy(like, like, small_send.at[n], small_recv.at[n], sibling).wait()
        return jnp.sum(small[n][...], axis=0)

    def send_away(s):
        if s > 1:
            sent(s, 0)
        for q in range(4):
            rows = pl.ds(q * H, H)
            push(away.at[s, rows], core_in.at[s, rows], s, 0, 0, sibling)

    def chain(p, n, high, low):
        s = 2 * n + p
        (a, a_devices), (b, b_devices) = [((y, ys), (zl, zls)), ((zl, zls), (y, ys))][p]

        def again(*phases):
            for phase in phases if n else ():
                sent(s, phase)

        yield
        if n:
            own_back_terms(p)
        again(1)
        arrived(core_in.at[s], s, 0)
        own[s] = own[s] + core_in[s]
        for j in (2, 1, 3):
            push(own.at[s, rows_of((a + j) % 4 * H, H)], a_in.at[s, j - 1], s, 1, 1, a_devices[j - 1])
        again(2)
        yield
        mine = rows_of(a * H, H)
        arrived(a_in.at[s], s, 1)
        b_in[s, b] = (own[s, mine] + a_in[s, 0]) + (a_in[s, 1] + a_in[s, 2])
        for j in (2, 1, 3):
            push(b_in.at[s, b], b_in.at[s, b], s, 2, 2, b_devices[j - 1])
        again(3, 4)
        yield
        arrived(a_in.at[s], s, 2)
        here = rows_of(k * 256 + a * H, H)
        full_c[s, here] = (b_in[s, 0] + b_in[s, 1]) + (b_in[s, 2] + b_in[s, 3])
        for j in (2, 1, 3):
            push(full_c.at[s, here], full_c.at[s, here], s, 3, 3 + j - 1, a_devices[j - 1])
        push(full_c.at[s, here], full_c.at[s, here], s, 4, 6, sibling)
        yield
        for j in (1, 3, 2):
            there = rows_of(k * 256 + (a + 4 - j) % 4 * H, H)
            arrived(full_c.at[s, there], s, 3 + j - 1)
            push(full_c.at[s, there], full_c.at[s, there], s, 4, 6, sibling)
        mine, his = rows_of(k * 512, 512), rows_of((1 - k) * 512, 512)

        def half(base):
            return jnp.concatenate([operand(full_c[s, rows_of(base * 256 + q * H, H)]) for q in range(4)], axis=0)

        term = half(k)
        for q in range(4):
            rows = pl.ds(q * Q, Q)
            part[s, rows] = dot(high[rows, mine], term) + dot(low[rows, mine], term)
        again(5)
        yield
        arrived(full_c.at[s, rows_of((1 - k) * 256, 256)], s, 6)
        term = half(1 - k)
        slots = [zh_out.at[s, 0], zh_out.at[s, 2], zh_out.at[s, 3], zh_out.at[s, 4]]

        def finish(j):
            rows = rows_of((x + j) % 4 * Q, Q)
            slots[j][...] = fold(part[s, rows] + (dot(high[rows, his], term) + dot(low[rows, his], term)))

        for j in (2, 1, 3):
            finish(j)
        for j in (2, 1, 3):
            push(slots[j], x_in.at[s, j - 1], s, 5, 7, xs[j - 1])
        finish(0)
        again(6, 7)
        yield
        arrived(x_in.at[s], s, 7)
        zh_out[s, 0] = (zh_out[s, 0] + x_in[s, 0]) + (x_in[s, 1] + x_in[s, 2])
        first, second = pl.ds(0, H // 2), pl.ds(H // 2, H // 2)
        push(zh_out.at[s, 0, first], zh_in1.at[s, 0], s, 6, 8, zh_a)
        push(zh_out.at[s, 0, second], zh_in1.at[s, 1], s, 6, 9, zh_b)
        yield
        arrived(zh_in1.at[s, 0], s, 8)
        zh_out[s, 1, first] = zh_out[s, 0, first] + zh_in1[s, 0]
        push(zh_out.at[s, 1, first], zh_in2.at[s, 0], s, 7, 10, zh_b)
        arrived(zh_in1.at[s, 1], s, 9)
        zh_out[s, 1, second] = zh_out[s, 0, second] + zh_in1[s, 1]
        push(zh_out.at[s, 1, second], zh_in2.at[s, 1], s, 7, 10, zh_a)
        again(8)
        yield
        here = rows_of(x * H, H)
        arrived(zh_in2.at[s], s, 10)
        full_r[s, here] = zh_out[s, 1] + zh_in2[s].reshape(H, T)
        if s == 3:
            yield
        for j in (2, 1, 3):
            push(full_r.at[s, here], full_r.at[s, here], s, 8, 11, xs[j - 1])
        yield
        arrived(x_in.at[s], s, 11)

    def back_terms(p, base):
        b = jnp.concatenate([operand(full_r[p, q * H : (q + 1) * H]) for q in range(4)], axis=0)
        for q in range(4):
            rows = rows_of(base * 512 + q * Q, Q)
            yield q, fold(dot(kth[rows, :], b) + dot(ktl[rows, :], b))

    def own_back_terms(p):
        for q, term in back_terms(p, k):
            own[2 + p, q * H : (q + 1) * H] = term

    def whole(p):
        yield from chain(p, 0, kh, kl)
        for q, term in back_terms(p, 1 - k):
            away[2 + p, q * H : (q + 1) * H] = term
        send_away(2 + p)
        yield from chain(p, 1, rth, rtl)

    def kernel_block(e):
        def run():
            if e == 0:
                loads[3].wait()
                loads[4].wait()
            cols = slice(e * 256, (e + 1) * 256)
            a, b = points[...], centers[cols, :]
            a_sq = jnp.sum(a * a, axis=1, keepdims=True)
            b_sq = across(jnp.ones((8, b.shape[1]), F32), b * b)[0:1]
            block = jnp.exp(-0.5 * ((a_sq + b_sq) - 2.0 * across(a, b)))
            kh[:, cols], kl[:, cols] = split(block)
            kth[cols, :], ktl[cols, :] = split(block.T)

        return run

    def factor_block(e):
        def run():
            cols = slice(e * 256, (e + 1) * 256)
            rth[:, cols], rtl[:, cols] = split(factor[cols, :].T)

        return run

    def norm(a):
        return jnp.sum(a * a, axis=0, keepdims=True)

    def first_norms():
        loads[5].wait()
        squares = [norm(full_r[p]) for p in (0, 1)]
        squares = [a + swap(a) for a in squares]
        predicted = jnp.where(first_lanes(1), squares[0], squares[1])
        small_start(0, jnp.concatenate([norm(residual[...]), norm(direction[...]), predicted], axis=1))

    loads[0].wait()
    pair = jnp.concatenate(split(direction[...]), axis=1)

    def mapped(base, target):
        for q in range(4):
            high, low = split(factor[rows_of(base * 512 + q * Q, Q), :])
            both = dot(high, pair) + dot(low, pair)
            both = both[:, :T] + both[:, T:]
            for p in (0, 1):
                target[p, q * H : (q + 1) * H] = pack(both, p)

    loads[1].wait()
    mapped(1 - k, away)
    pl.semaphore_wait(barrier, len(peers))
    for p in (0, 1):
        send_away(p)
    loads[2].wait()
    mapped(k, own)

    chains = [whole(0), whole(1)]
    extra = {
        1: [kernel_block(0), kernel_block(1)],
        2: [kernel_block(2), kernel_block(3)],
        6: [factor_block(0), factor_block(1)],
        7: [factor_block(2), factor_block(3)],
        10: [first_norms],
    }
    for step in range(18):
        for p in (0, 1):
            next(chains[p])
        for run in extra.get(step, []):
            run()

    sums = small_end(0)
    norm_now = sums[:, :T]
    step_size = norm_now / (sums[:, 2 * T :] + ridge_weight * sums[:, T : 2 * T])
    quarter, packed = rows_of(x * Q, Q), rows_of(x * H, H)
    fresh = residual[quarter, :] - step_size * (
        unpack(full_r[2, packed], full_r[3, packed]) + ridge_weight * direction[quarter, :]
    )
    small_x[x] = norm(fresh)
    for device in xs:
        copy(small_x.at[x], small_x.at[x], small_send.at[2], small_recv.at[2], device).start()
    next(chains[1])
    line[0] = step_size
    outs = [pltpu.make_async_copy(line.at[0], step_out, local.at[6])]
    outs[0].start()
    like = small_x.at[pl.ds(0, 3)]
    copy(like, like, small_send.at[2], small_recv.at[2], sibling).wait()
    small_start(1, jnp.sum(small_x[...], axis=0))
    for p in (0, 1):
        for unused in chains[p]:
            pass
    for q in range(4):
        packed = pl.ds(q * H, H)
        image[q * Q : (q + 1) * Q] = unpack(full_r[2, packed], full_r[3, packed])
    outs.append(pltpu.make_async_copy(image, image_, local.at[7]))
    outs[1].start()
    for p in (0, 1):
        for phase in range(9):
            sent(2 + p, phase)
    for out in outs:
        out.wait()
    line[1] = small_end(1) / norm_now
    last = pltpu.make_async_copy(line.at[1], ratio_out, local.at[8])
    last.start()
    last.wait()


def body(points, centers, factor, solution_, residual, direction):
    anywhere = pl.BlockSpec(memory_space=pl.ANY)
    dma = pltpu.SemaphoreType.DMA
    v = lambda *shape: pltpu.VMEM(shape, F32)
    h = lambda *shape: pltpu.VMEM(shape, BF16)
    image, step_size, ratio = pl.pallas_call(
        kernel,
        name="cg_iteration",
        out_shape=(jax.ShapeDtypeStruct(direction.shape, F32), jax.ShapeDtypeStruct((1, T), F32), jax.ShapeDtypeStruct((1, T), F32)),
        in_specs=[anywhere] * 5,
        out_specs=(anywhere,) * 3,
        scratch_shapes=[
            v(512, 256), v(1024, 256), v(1024, 512), v(512, T), v(512, T), v(512, T),
            v(4, 256, T), v(4, 256, T), v(4, 256, T), v(4, 3, H, T), v(4, 4, H, T), v(4, 512, T),
            v(4, 512, T), v(4, 3, H, T), v(4, 5, H, T), v(4, 2, H // 2, T), v(4, 2, H // 2, T), v(4, 256, T),
            h(512, 1024), h(512, 1024), h(1024, 512), h(1024, 512), h(512, 1024), h(512, 1024),
            v(32, 1, 3 * T), v(32, 1, T), v(4, 1, T), v(2, 1, T),
            dma((2, 9)), dma((4, 12)), dma((3,)), dma((3,)), dma((9,)),
        ],
        compiler_params=pltpu.CompilerParams(collective_id=0, has_side_effects=True, vmem_limit_bytes=60 * 2**20),
    )(points, centers, factor, residual, direction)
    new_solution = solution_ + step_size * direction
    new_residual = residual - step_size * (image + ridge_weight * direction)
    return new_solution, new_residual, new_residual + ratio * direction


def solution(mesh):
    return jax.shard_map(
        body,
        mesh=mesh,
        in_specs=(
            P("rows", None),
            P("cols", None),
            P("cols", "rows"),
            P("rows", None),
            P("rows", None),
            P("rows", None),
        ),
        out_specs=(P("rows", None), P("rows", None), P("rows", None)),
        check_vma=False,
    )
```
